256 devices in a mesh: dp: 32 (over y_lo, z, core), ctx: 8 (over y_hi, x).
Axes of the slice: x: 4, y: 4 (y_hi: 2, y_lo: 2; y = y_hi * 2 + y_lo), z: 8, core: 2. Of those that a mesh axis runs over, the one named last changes fastest.
Arguments:
- query_proj: bfloat16 [64, 512, 4096], P('dp', 'ctx'), may hold values from -5 to 5
- key_proj: bfloat16 [64, 512, 1024], P('dp', 'ctx'), may hold values from -5 to 5
- value_proj: bfloat16 [64, 512, 1024], P('dp', 'ctx'), may hold values from -6 to 6
- grad_attn: bfloat16 [64, 512, 4096], P('dp', 'ctx'), may hold values from -6 to 6
- doc_lengths: int32 [64, 8], replicated, may hold values from 1 to 128, 512 in all within a row
- mask_tiles: int32 [64, 8, 8], replicated, may hold values from 0 to 1, as said below
- pair_flags: int32 [32], replicated, may hold values from 0 to 1, as said below
Outputs:
- attn_out: bfloat16 [64, 512, 4096], P('dp', 'ctx')
- grad_query: bfloat16 [64, 512, 4096], P('dp', 'ctx')
- grad_key: bfloat16 [64, 512, 1024], P('dp', 'ctx')
- grad_value: bfloat16 [64, 512, 1024], P('dp', 'ctx')
The draws below stay inside these ranges and needn't reach their ends.
Inputs may be any that keep to these rules, and one draw needn't show every extreme that they name: `doc_lengths`: each row sums to 512. mask_tiles[n, t, t] = 1 for every sequence n and tile t. pair_flags[r] = pair_flags[r XOR (16)] for every r.
All inputs are finite; a program needn't handle non-finite values.
Results may differ from the reference program's by a relative error of at most 0.03.
Values may be sent and summed in bfloat16 or wider, within the bound.
A program may use at most 128 MiB of HBM per device.

```python
import math
import jax
import jax.numpy as jnp
import numpy as np
from jax import lax

QUERY_HEADS = 32
KEY_VALUE_HEADS = 8
HEAD_SIZE = 128
TILE = 64
NDOC = 8
QF = 4096
KF = 1024
PACKED_LENGTH = 512
NT = 8
SEQUENCE_COUNT = 64


def draw_query_proj(key, part):
    base_offset = jnp.clip(jax.random.normal(jax.random.fold_in(key, 1), (SEQUENCE_COUNT, PACKED_LENGTH, QUERY_HEADS * HEAD_SIZE), jnp.float32), -4.0, 4.0)
    return base_offset.astype(jnp.bfloat16)


def draw_key_proj(key, part):
    base_offset = jnp.clip(jax.random.normal(jax.random.fold_in(key, 2), (SEQUENCE_COUNT, PACKED_LENGTH, KEY_VALUE_HEADS * HEAD_SIZE), jnp.float32), -4.0, 4.0)
    return base_offset.astype(jnp.bfloat16)


def draw_mask_tiles(key, part):
    opened = jax.random.randint(jax.random.fold_in(key, 3), (SEQUENCE_COUNT, NT, NT), 0, 2)
    diagonal = jnp.arange(NT)[:, None] == jnp.arange(NT)[None, :]
    return jnp.where(diagonal[None, :, :], 1, opened).astype(jnp.int32)


def draw_pair_flags(key, part):
    half = SEQUENCE_COUNT // 4
    flags = jax.random.randint(jax.random.fold_in(key, 4), (half,), 0, 2)
    chosen = jax.random.randint(jax.random.fold_in(key, 5), (), 0, half)
    flags = jnp.where(jnp.arange(half) == chosen, 1, flags)
    return jnp.concatenate([flags, flags]).astype(jnp.int32)


def block_levels(own_key, extent, pieces, least, top_value):
    def one(dim, blocks):
        draws = jax.random.uniform(jax.random.fold_in(jax.random.fold_in(own_key, 6), dim), (blocks,), jnp.float32, least / len(pieces), top_value / len(pieces))
        return jnp.repeat(jnp.exp(draws), extent[dim] // blocks).reshape((-1,) + (1,) * (len(extent) - dim - 1))

    gain = one(*pieces[0])
    for cut in pieces[1:]:
        gain = gain * one(*cut)
    return gain


def split_up(number_of, total, reach, skew):
    weights = [(1 << 20) // math.isqrt(standing ** skew) + 1 for standing in range(2, number_of + 1)]
    rest, holding = total - reach - (number_of - 1), [1] * (number_of - 1)
    while rest > 0:
        candidates = [i for i in range(number_of - 1) if holding[i] < reach]
        pool, budget = sum([weights[i] for i in candidates]), rest
        for i in candidates:
            extra = min(reach - holding[i], max(1, budget * weights[i] // pool), rest)
            holding[i] = holding[i] + extra
            rest = rest - extra
    return np.array([reach] + holding)


def uneven(rng, amount, total, bound, slope):
    if amount == 2:
        one = jax.random.randint(rng, (), max(1, total - bound), min(bound, total - 1) + 1)
        return jnp.stack([one, total - one])
    tallies = jnp.asarray(split_up(amount, total, bound, slope), jnp.int32)
    twos = (amount - 1) // 2
    giver, sink = tallies[1:1 + 2 * twos:2], tallies[2:2 + 2 * twos:2]
    slack = jnp.minimum(giver - 1, bound - sink)
    moved = jax.random.randint(jax.random.fold_in(rng, 1), (twos,), 0, 1 << 20) % (slack + 1)
    tallies = tallies.at[1:1 + 2 * twos:2].set(giver - moved).at[2:2 + 2 * twos:2].set(sink + moved)
    return tallies[jax.random.permutation(jax.random.fold_in(rng, 2), amount)]


def bell_draw(own_key, extent, scale, reach, shards=(), kind=jnp.bfloat16):
    factor_of = block_levels(own_key, extent, shards, -0.22, 0.18) if shards else 1.0
    entries = jax.random.normal(own_key, extent, jnp.float32) * scale * factor_of
    return jnp.minimum(jnp.maximum(entries, -reach), reach).astype(kind)


def setup_inputs(seed: int = 0) -> dict:
    key_list = jax.random.split(jax.random.key(seed), 8)
    query_proj = draw_query_proj(jax.random.fold_in(key_list[7], 71), 0)
    key_proj = draw_key_proj(jax.random.fold_in(key_list[7], 71), 0)
    value_proj = bell_draw(key_list[2], (SEQUENCE_COUNT, PACKED_LENGTH, KF), 1.0, 6.0, ((0, 32), (1, 8)))
    grad_attn = bell_draw(key_list[3], (SEQUENCE_COUNT, PACKED_LENGTH, QF), 1.0, 6.0, ((0, 32), (1, 8)))
    doc_lengths = jax.vmap(lambda own: uneven(own, NDOC, PACKED_LENGTH, PACKED_LENGTH // 4, 2))(jax.random.split(key_list[4], SEQUENCE_COUNT)).reshape((SEQUENCE_COUNT, NDOC)).astype(jnp.int32)
    mask_tiles = draw_mask_tiles(jax.random.fold_in(key_list[7], 71), 0)
    pair_flags = draw_pair_flags(jax.random.fold_in(key_list[7], 71), 0)
    return dict(query_proj=query_proj, key_proj=key_proj, value_proj=value_proj, grad_attn=grad_attn, doc_lengths=doc_lengths, mask_tiles=mask_tiles, pair_flags=pair_flags)


def sequence_pass(query_rows, sequence_keys, sequence_values, sequence_gradients, lengths, tile_table):
    length_total = query_rows.shape[0]
    group_ratio = QUERY_HEADS // KEY_VALUE_HEADS
    scale = HEAD_SIZE ** -0.5
    positions = jnp.arange(length_total, dtype=jnp.int32)
    ends = jnp.cumsum(lengths.astype(jnp.int32))[:-1].astype(jnp.int32)
    doc_ids = jnp.sum((positions[:, None] >= ends[None, :]).astype(jnp.int32), axis=1)
    tile_map = jnp.repeat(jnp.repeat(tile_table, TILE, axis=0), TILE, axis=1) == 1
    allowed = (positions[None, :] <= positions[:, None]) & ((doc_ids[None, :] == doc_ids[:, None]) | (doc_ids[None, :] == 0)) & tile_map
    heads_of_queries = query_rows.reshape(length_total, KEY_VALUE_HEADS, group_ratio, HEAD_SIZE).astype(jnp.float32)
    heads_of_keys = sequence_keys.reshape(length_total, KEY_VALUE_HEADS, HEAD_SIZE).astype(jnp.float32)
    heads_of_values = sequence_values.reshape(length_total, KEY_VALUE_HEADS, HEAD_SIZE).astype(jnp.float32)
    head_gradients = sequence_gradients.reshape(length_total, KEY_VALUE_HEADS, group_ratio, HEAD_SIZE).astype(jnp.float32)
    scores = jnp.einsum("igrd,jgd->grij", heads_of_queries, heads_of_keys) * scale
    scores = jnp.where(allowed, scores, -1e30)
    peak = jnp.max(scores, axis=-1, keepdims=True)
    expd = jnp.where(allowed, jnp.exp(scores - peak), 0.0)
    probs = expd / jnp.sum(expd, axis=-1, keepdims=True)
    probs_b = probs.astype(jnp.bfloat16).astype(jnp.float32)
    attn = jnp.einsum("grij,jgd->igrd", probs_b, heads_of_values).astype(jnp.bfloat16)
    delta = jnp.transpose(jnp.sum(head_gradients * attn.astype(jnp.float32), axis=-1), (1, 2, 0))
    value_gradient = jnp.einsum("grij,igrd->jgd", probs_b, head_gradients)
    dprobs = jnp.einsum("igrd,jgd->grij", head_gradients, heads_of_values)
    dscores = (probs * (dprobs - delta[..., None]) * scale).astype(jnp.bfloat16).astype(jnp.float32)
    grad_q = jnp.einsum("grij,jgd->igrd", dscores, heads_of_keys)
    key_gradient = jnp.einsum("grij,igrd->jgd", dscores, heads_of_queries)
    return (attn.reshape(length_total, QUERY_HEADS * HEAD_SIZE),
            grad_q.astype(jnp.bfloat16).reshape(length_total, QUERY_HEADS * HEAD_SIZE),
            key_gradient.astype(jnp.bfloat16).reshape(length_total, KEY_VALUE_HEADS * HEAD_SIZE),
            value_gradient.astype(jnp.bfloat16).reshape(length_total, KEY_VALUE_HEADS * HEAD_SIZE))


def reference(query_proj, key_proj, value_proj, grad_attn, doc_lengths, mask_tiles, pair_flags):
    ranks = SEQUENCE_COUNT // 2
    seq_index = jnp.arange(SEQUENCE_COUNT, dtype=jnp.int32)
    owner = (seq_index // 2).astype(jnp.int32)
    partner = jnp.bitwise_xor(owner, ranks // 2).astype(jnp.int32)
    flags = jnp.take(pair_flags, owner, axis=0)
    order = jnp.where((seq_index % 2 == 1) & (flags == 1), 2 * partner + 1, seq_index).astype(jnp.int32)

    def one_sequence(index):
        return sequence_pass(query_proj[index], key_proj[index], value_proj[index], grad_attn[index], doc_lengths[index], mask_tiles[index])

    attn_out, grad_query, grad_key, grad_value = lax.map(one_sequence, order)
    return (attn_out, grad_query, grad_key, grad_value)
```

```python
import functools
import math

import jax
import jax.numpy as jnp
from jax import lax
from jax.experimental import pallas as pl
from jax.experimental.pallas import tpu as pltpu
from jax.sharding import PartitionSpec as P

MESH = pl.DeviceIdType.MESH
HEAD = 128
RATIO = 4
CTX = 8
ROWS = 64
LENGTH = 512
BLOCK = 128
CHUNKS = 2
HEADS_PER_CHUNK = RATIO // CHUNKS
WIDTH = HEADS_PER_CHUNK * HEAD
PEERS = 2 * CTX
SCALE = HEAD ** (-0.5)
EXP2_SCALE = SCALE / math.log(2.0)
COLUMN_BLOCKS = ((0,), (0, 1), (0, 1, 2), (0, 2, 3))
BIAS_START = (0, 128, 384, 768)
BIAS_ROWS = 1152
NT_DIMS = (((1,), (1,)), ((), ()))
TN_DIMS = (((0,), (0,)), ((), ()))
NN_DIMS = (((1,), (0,)), ((), ()))


def mm(a, b, dims):
    return lax.dot_general(a, b, dims, preferred_element_type=jnp.float32)


def take_columns(ref, slot, b):
    blocks = COLUMN_BLOCKS[b]
    if blocks == tuple(range(len(blocks))):
        return ref[slot, 0 : BLOCK * len(blocks), :]
    return jnp.concatenate(
        [ref[slot, BLOCK * cb : BLOCK * (cb + 1), :] for cb in blocks], axis=0
    )


def kernel(
    q_in, k_in, v_in, g_in, lengths, tiles, flags,
    attn_out, gq_out, gk_out, gv_out,
    kbuf, vbuf, abuf, gqbuf, dk, dv, gkbuf, gvbuf, bias,
    recv_q, recv_g, recv_kv, send_q, send_g, send_kv,
    recv_out, send_a, send_gq, send_gkv,
    *chunk_bufs,
):
    qbuf, gbuf = chunk_bufs[:CHUNKS], chunk_bufs[CHUNKS:]
    dp = lax.axis_index("dp")
    c = lax.axis_index("ctx")
    half = lax.axis_size("dp") // 2
    low = dp // half
    zc = dp % half

    def peer(k):
        s = (low + k // CTX) % 2
        h = (c + k % CTX) % CTX
        return s, h, {"dp": s * half + zc, "ctx": h}

    barrier = pltpu.get_barrier_semaphore()

    @pl.loop(1, PEERS)
    def _(k):
        _, _, device = peer(k)
        pl.semaphore_signal(barrier, inc=1, device_id=device, device_id_type=MESH)

    pl.semaphore_wait(barrier, PEERS - 1)

    my_rows = pl.ds(pl.multiple_of(c * ROWS, ROWS), ROWS)

    def in_copies(j, s, h):
        wide = pl.ds(pl.multiple_of(h * (RATIO * HEAD) + j * WIDTH, WIDTH), WIDTH)
        out = [
            (q_in.at[s, :, wide], qbuf[j].at[low, my_rows, :], send_q.at[j], recv_q.at[j]),
            (g_in.at[s, :, wide], gbuf[j].at[low, my_rows, :], send_g.at[j], recv_g.at[j]),
        ]
        if j == 0:
            thin = pl.ds(pl.multiple_of(h * HEAD, HEAD), HEAD)
            out = [
                (k_in.at[s, :, thin], kbuf.at[low, my_rows, :], send_kv.at[0], recv_kv.at[0]),
                (v_in.at[s, :, thin], vbuf.at[low, my_rows, :], send_kv.at[1], recv_kv.at[1]),
            ] + out
        return out

    def start_remote(copies, device):
        for src, dst, send, recv in copies:
            pltpu.make_async_remote_copy(
                src_ref=src, dst_ref=dst, send_sem=send, recv_sem=recv,
                device_id=device, device_id_type=MESH,
            ).start()

    def start_local(copies):
        for src, dst, _, recv in copies:
            pltpu.make_async_copy(src, dst, recv).start()

    for j in range(CHUNKS):

        @pl.loop(1, PEERS)
        def _(k, j=j):
            s, h, device = peer(k)
            start_remote(in_copies(j, s, h), device)

        start_local(in_copies(j, low, c))

    flag = jnp.where(flags[dp] == 1, 1, 0) * low
    lane = lax.broadcasted_iota(jnp.int32, (BLOCK, BLOCK), 1)
    sub = lax.broadcasted_iota(jnp.int32, (BLOCK, BLOCK), 0)

    def source(slot):
        return slot + flag - 2 * slot * flag

    @pl.loop(0, 2)
    def _(slot):
        seq = 2 * (source(slot) * half + zc) + low
        ends = []
        total = lengths[seq, 0]
        for d in range(1, 8):
            ends.append(total)
            total = total + lengths[seq, d]
        for b in range(4):
            row = lane + BLOCK * b
            row_doc = sum((row >= e).astype(jnp.int32) for e in ends)
            for n, cb in enumerate(COLUMN_BLOCKS[b]):
                col = sub + BLOCK * cb
                col_doc = sum((col >= e).astype(jnp.int32) for e in ends)
                first = jnp.where(lane < 64, tiles[seq, 2 * b, 2 * cb], tiles[seq, 2 * b + 1, 2 * cb])
                second = jnp.where(
                    lane < 64, tiles[seq, 2 * b, 2 * cb + 1], tiles[seq, 2 * b + 1, 2 * cb + 1]
                )
                tile = jnp.where(sub < 64, first, second)
                allowed = (col <= row) & ((col_doc == row_doc) | (col_doc == 0)) & (tile == 1)
                at = BIAS_START[b] + BLOCK * n
                bias[slot, at : at + BLOCK, :] = jnp.where(allowed, 0.0, -1e30)

    dk[...] = jnp.zeros_like(dk)
    dv[...] = jnp.zeros_like(dv)

    pltpu.make_async_copy(kbuf, kbuf, recv_kv.at[0]).wait()
    pltpu.make_async_copy(vbuf, vbuf, recv_kv.at[1]).wait()

    def add_columns(ref, slot, b, value):
        for n, cb in enumerate(COLUMN_BLOCKS[b]):
            ref[slot, BLOCK * cb : BLOCK * (cb + 1), :] += value[BLOCK * n : BLOCK * (n + 1)]

    def out_copies(j, s, h):
        rows = pl.ds(pl.multiple_of(h * ROWS, ROWS), ROWS)
        wide = pl.ds(pl.multiple_of(c * (RATIO * HEAD) + j * WIDTH, WIDTH), WIDTH)
        return [
            (abuf.at[j, s, rows, :], attn_out.at[low, :, wide], send_a.at[j], recv_out.at[0]),
            (gqbuf.at[j, s, rows, :], gq_out.at[low, :, wide], send_gq.at[j], recv_out.at[1]),
        ]

    def kv_copies(s, h):
        rows = pl.ds(pl.multiple_of(h * ROWS, ROWS), ROWS)
        thin = pl.ds(pl.multiple_of(c * HEAD, HEAD), HEAD)
        return [
            (gkbuf.at[s, rows, :], gk_out.at[low, :, thin], send_gkv.at[0], recv_out.at[2]),
            (gvbuf.at[s, rows, :], gv_out.at[low, :, thin], send_gkv.at[1], recv_out.at[3]),
        ]

    for j in range(CHUNKS):
        pltpu.make_async_copy(qbuf[j], qbuf[j], recv_q.at[j]).wait()
        pltpu.make_async_copy(gbuf[j], gbuf[j], recv_g.at[j]).wait()

        @pl.loop(0, 2)
        def _(slot, j=j):
            u = source(slot)
            for b in range(4):
                rows = slice(BLOCK * b, BLOCK * (b + 1))
                n_cols = BLOCK * len(COLUMN_BLOCKS[b])
                keys = take_columns(kbuf, u, b)
                values = take_columns(vbuf, u, b)
                heads = [slice(HEAD * h, HEAD * (h + 1)) for h in range(HEADS_PER_CHUNK)]
                queries = jnp.concatenate([qbuf[j][u, rows, h] for h in heads], axis=0)
                grads = jnp.concatenate([gbuf[j][u, rows, h] for h in heads], axis=0)
                mask = bias[slot, BIAS_START[b] : BIAS_START[b] + n_cols, :]
                mask = jnp.concatenate([mask] * HEADS_PER_CHUNK, axis=1)
                scores = mm(keys, queries, NT_DIMS) + mask
                peak = jnp.max(scores, axis=0, keepdims=True)
                expd = jnp.exp2((scores - peak) * EXP2_SCALE)
                probs = expd * (1.0 / jnp.sum(expd, axis=0, keepdims=True))
                probs_b = probs.astype(jnp.bfloat16)
                dprobs = mm(values, grads, NT_DIMS)
                delta = jnp.sum(probs * dprobs, axis=0, keepdims=True)
                dscores = (probs * (dprobs - delta)).astype(jnp.bfloat16)
                attn = mm(probs_b, values, TN_DIMS).astype(jnp.bfloat16)
                gq = (mm(dscores, keys, TN_DIMS) * SCALE).astype(jnp.bfloat16)
                for n, h in enumerate(heads):
                    abuf[j, slot, rows, h] = attn[BLOCK * n : BLOCK * (n + 1)]
                    gqbuf[j, slot, rows, h] = gq[BLOCK * n : BLOCK * (n + 1)]
                add_columns(dv, slot, b, mm(probs_b, grads, NN_DIMS))
                add_columns(dk, slot, b, mm(dscores, queries, NN_DIMS))

        if j == CHUNKS - 1:
            gkbuf[...] = (dk[...] * SCALE).astype(jnp.bfloat16)
            gvbuf[...] = dv[...].astype(jnp.bfloat16)

        @pl.loop(1, PEERS)
        def _(k, j=j):
            s, h, device = peer(k)
            start_remote(out_copies(j, s, h), device)
            if j == CHUNKS - 1:
                start_remote(kv_copies(s, h), device)

        start_local(out_copies(j, low, c))
        if j == CHUNKS - 1:
            start_local(kv_copies(low, c))

    sent = pl.ds(0, LENGTH - ROWS // 2)
    for j in range(CHUNKS):
        for buf, sem in (
            (qbuf[j], send_q), (gbuf[j], send_g), (abuf.at[j], send_a), (gqbuf.at[j], send_gq)
        ):
            part = buf.at[:, sent, :]
            pltpu.make_async_copy(part, part, sem.at[j]).wait()
    for buf, sem in (
        (kbuf, send_kv.at[0]), (vbuf, send_kv.at[1]), (gkbuf, send_gkv.at[0]), (gvbuf, send_gkv.at[1])
    ):
        part = buf.at[:, sent, :]
        pltpu.make_async_copy(part, part, sem).wait()
    for n, ref in enumerate((attn_out, gq_out, gk_out, gv_out)):
        pltpu.make_async_copy(ref, ref, recv_out.at[n]).wait()


def shards(query_proj, key_proj, value_proj, grad_attn, doc_lengths, mask_tiles, pair_flags):
    bf16, f32 = jnp.bfloat16, jnp.float32
    dma = pltpu.SemaphoreType.DMA
    anywhere = pl.BlockSpec(memory_space=pl.ANY)
    scalars = pl.BlockSpec(memory_space=pltpu.SMEM)
    wide = pltpu.VMEM((CHUNKS, 2, LENGTH, WIDTH), bf16)
    chunk = pltpu.VMEM((2, LENGTH, WIDTH), bf16)
    thin = pltpu.VMEM((2, LENGTH, HEAD), bf16)
    total = pltpu.VMEM((2, LENGTH, HEAD), f32)
    return pl.pallas_call(
        kernel,
        out_shape=tuple(
            jax.ShapeDtypeStruct(a.shape, bf16)
            for a in (query_proj, query_proj, key_proj, value_proj)
        ),
        in_specs=[anywhere] * 4 + [scalars] * 3,
        out_specs=(anywhere,) * 4,
        scratch_shapes=[
            thin, thin, wide, wide, total, total, thin, thin,
            pltpu.VMEM((2, BIAS_ROWS, BLOCK), f32),
            dma((CHUNKS,)), dma((CHUNKS,)), dma((2,)),
            dma((CHUNKS,)), dma((CHUNKS,)), dma((2,)),
            dma((4,)), dma((CHUNKS,)), dma((CHUNKS,)), dma((2,)),
            *[chunk] * (2 * CHUNKS),
        ],
        compiler_params=pltpu.CompilerParams(
            collective_id=0, has_side_effects=True, vmem_limit_bytes=48 * 2**20
        ),
    )(query_proj, key_proj, value_proj, grad_attn, doc_lengths, mask_tiles, pair_flags)


def solution(mesh):
    split = P("dp", "ctx", None)
    return jax.shard_map(
        shards,
        mesh=mesh,
        in_specs=(split,) * 4 + (P(),) * 3,
        out_specs=(split,) * 4,
        check_vma=False,
    )
```

```python
import functools
import math

import jax
import jax.numpy as jnp
from jax import lax
from jax.experimental import pallas as pl
from jax.experimental.pallas import tpu as pltpu
from jax.sharding import PartitionSpec as P

MESH = pl.DeviceIdType.MESH
HEAD = 128
RATIO = 4
CTX = 8
ROWS = 64
LENGTH = 512
BLOCK = 128
CHUNKS = 2
HEADS_PER_CHUNK = RATIO // CHUNKS
WIDTH = HEADS_PER_CHUNK * HEAD
PEERS = 2 * CTX
ORDER = (
    (1, 1), (3, 3), (2, 2), (0, 1), (1, 0), (3, 2), (2, 3), (0, 2),
    (3, 1), (1, 2), (2, 0), (0, 3), (1, 3), (3, 0), (2, 1),
)
SCALE = HEAD ** (-0.5)
EXP2_SCALE = SCALE / math.log(2.0)
COLUMN_BLOCKS = ((0,), (0, 1), (0, 1, 2), (0, 2, 3))
BIAS_START = (0, 128, 384, 768)
BIAS_ROWS = 1152
NT_DIMS = (((1,), (1,)), ((), ()))
TN_DIMS = (((0,), (0,)), ((), ()))
NN_DIMS = (((1,), (0,)), ((), ()))


def mm(a, b, dims):
    return lax.dot_general(a, b, dims, preferred_element_type=jnp.float32)


def take_columns(ref, slot, b):
    blocks = COLUMN_BLOCKS[b]
    if blocks == tuple(range(len(blocks))):
        return ref[slot, 0 : BLOCK * len(blocks), :]
    return jnp.concatenate(
        [ref[slot, BLOCK * cb : BLOCK * (cb + 1), :] for cb in blocks], axis=0
    )


def kernel(
    q_in, k_in, v_in, g_in, lengths, tiles, flags,
    attn_out, gq_out, gk_out, gv_out,
    kbuf, vbuf, abuf, gqbuf, dk, dv, gkbuf, gvbuf, bias,
    recv_q, recv_g, recv_kv, send_q, send_g, send_kv,
    recv_out, send_a, send_gq, send_gkv,
    *chunk_bufs,
):
    qbuf, gbuf = chunk_bufs[:CHUNKS], chunk_bufs[CHUNKS:]
    dp = lax.axis_index("dp")
    c = lax.axis_index("ctx")
    half = lax.axis_size("dp") // 2
    low = dp // half
    zc = dp % half

    def peer(step):
        dx, dy = step
        s = (low + dy % 2) % 2
        h = (c // 4 + dy // 2) % 2 * 4 + (c % 4 + dx) % 4
        return s, h, {"dp": s * half + zc, "ctx": h}

    barrier = pltpu.get_barrier_semaphore()

    for step in ORDER:
        _, _, device = peer(step)
        pl.semaphore_signal(barrier, inc=1, device_id=device, device_id_type=MESH)

    pl.semaphore_wait(barrier, PEERS - 1)

    my_rows = pl.ds(pl.multiple_of(c * ROWS, ROWS), ROWS)

    def in_copies(j, s, h):
        wide = pl.ds(pl.multiple_of(h * (RATIO * HEAD) + j * WIDTH, WIDTH), WIDTH)
        out = [
            (q_in.at[s, :, wide], qbuf[j].at[low, my_rows, :], send_q.at[j], recv_q.at[j]),
            (g_in.at[s, :, wide], gbuf[j].at[low, my_rows, :], send_g.at[j], recv_g.at[j]),
        ]
        if j == 0:
            thin = pl.ds(pl.multiple_of(h * HEAD, HEAD), HEAD)
            out = [
                (k_in.at[s, :, thin], kbuf.at[low, my_rows, :], send_kv.at[0], recv_kv.at[0]),
                (v_in.at[s, :, thin], vbuf.at[low, my_rows, :], send_kv.at[1], recv_kv.at[1]),
            ] + out
        return out

    def start_remote(copies, device):
        for src, dst, send, recv in copies:
            pltpu.make_async_remote_copy(
                src_ref=src, dst_ref=dst, send_sem=send, recv_sem=recv,
                device_id=device, device_id_type=MESH,
            ).start()

    def start_local(copies):
        for src, dst, _, recv in copies:
            pltpu.make_async_copy(src, dst, recv).start()

    for j in range(CHUNKS):
        for step in ORDER:
            s, h, device = peer(step)
            start_remote(in_copies(j, s, h), device)

        start_local(in_copies(j, low, c))

    flag = jnp.where(flags[dp] == 1, 1, 0) * low
    lane = lax.broadcasted_iota(jnp.int32, (BLOCK, BLOCK), 1)
    sub = lax.broadcasted_iota(jnp.int32, (BLOCK, BLOCK), 0)

    def source(slot):
        return slot + flag - 2 * slot * flag

    @pl.loop(0, 2)
    def _(slot):
        seq = 2 * (source(slot) * half + zc) + low
        ends = []
        total = lengths[0, seq]
        for d in range(1, 8):
            ends.append(total)
            total = total + lengths[d, seq]
        for b in range(4):
            row = lane + BLOCK * b
            row_doc = sum((row >= e).astype(jnp.int32) for e in ends)
            for n, cb in enumerate(COLUMN_BLOCKS[b]):
                col = sub + BLOCK * cb
                col_doc = sum((col >= e).astype(jnp.int32) for e in ends)
                first = jnp.where(lane < 64, tiles[2 * b, 2 * cb, seq], tiles[2 * b + 1, 2 * cb, seq])
                second = jnp.where(
                    lane < 64, tiles[2 * b, 2 * cb + 1, seq], tiles[2 * b + 1, 2 * cb + 1, seq]
                )
                tile = jnp.where(sub < 64, first, second)
                allowed = (col <= row) & ((col_doc == row_doc) | (col_doc == 0)) & (tile == 1)
                at = BIAS_START[b] + BLOCK * n
                bias[slot, at : at + BLOCK, :] = jnp.where(allowed, 0.0, -1e30)

    dk[...] = jnp.zeros_like(dk)
    dv[...] = jnp.zeros_like(dv)

    pltpu.make_async_copy(kbuf, kbuf, recv_kv.at[0]).wait()
    pltpu.make_async_copy(vbuf, vbuf, recv_kv.at[1]).wait()

    def add_columns(ref, slot, b, value):
        for n, cb in enumerate(COLUMN_BLOCKS[b]):
            ref[slot, BLOCK * cb : BLOCK * (cb + 1), :] += value[BLOCK * n : BLOCK * (n + 1)]

    def out_copies(j, s, h):
        rows = pl.ds(pl.multiple_of(h * ROWS, ROWS), ROWS)
        wide = pl.ds(pl.multiple_of(c * (RATIO * HEAD) + j * WIDTH, WIDTH), WIDTH)
        return [
            (abuf.at[j, s, rows, :], attn_out.at[low, :, wide], send_a.at[j], recv_out.at[0]),
            (gqbuf.at[j, s, rows, :], gq_out.at[low, :, wide], send_gq.at[j], recv_out.at[1]),
        ]

    def kv_copies(s, h):
        rows = pl.ds(pl.multiple_of(h * ROWS, ROWS), ROWS)
        thin = pl.ds(pl.multiple_of(c * HEAD, HEAD), HEAD)
        return [
            (gkbuf.at[s, rows, :], gk_out.at[low, :, thin], send_gkv.at[0], recv_out.at[2]),
            (gvbuf.at[s, rows, :], gv_out.at[low, :, thin], send_gkv.at[1], recv_out.at[3]),
        ]

    for j in range(CHUNKS):
        pltpu.make_async_copy(qbuf[j], qbuf[j], recv_q.at[j]).wait()
        pltpu.make_async_copy(gbuf[j], gbuf[j], recv_g.at[j]).wait()

        @pl.loop(0, 2)
        def _(slot, j=j):
            u = source(slot)
            for b in range(4):
                rows = slice(BLOCK * b, BLOCK * (b + 1))
                n_cols = BLOCK * len(COLUMN_BLOCKS[b])
                keys = take_columns(kbuf, u, b)
                values = take_columns(vbuf, u, b)
                heads = [slice(HEAD * h, HEAD * (h + 1)) for h in range(HEADS_PER_CHUNK)]
                queries = jnp.concatenate([qbuf[j][u, rows, h] for h in heads], axis=0)
                grads = jnp.concatenate([gbuf[j][u, rows, h] for h in heads], axis=0)
                mask = bias[slot, BIAS_START[b] : BIAS_START[b] + n_cols, :]
                mask = jnp.concatenate([mask] * HEADS_PER_CHUNK, axis=1)
                scores = mm(keys, queries, NT_DIMS) + mask
                peak = jnp.max(scores, axis=0, keepdims=True)
                expd = jnp.exp2((scores - peak) * EXP2_SCALE)
                probs = expd * (1.0 / jnp.sum(expd, axis=0, keepdims=True))
                probs_b = probs.astype(jnp.bfloat16)
                dprobs = mm(values, grads, NT_DIMS)
                delta = jnp.sum(probs * dprobs, axis=0, keepdims=True)
                dscores = (probs * (dprobs - delta)).astype(jnp.bfloat16)
                attn = mm(probs_b, values, TN_DIMS).astype(jnp.bfloat16)
                gq = (mm(dscores, keys, TN_DIMS) * SCALE).astype(jnp.bfloat16)
                for n, h in enumerate(heads):
                    abuf[j, slot, rows, h] = attn[BLOCK * n : BLOCK * (n + 1)]
                    gqbuf[j, slot, rows, h] = gq[BLOCK * n : BLOCK * (n + 1)]
                add_columns(dv, slot, b, mm(probs_b, grads, NN_DIMS))
                add_columns(dk, slot, b, mm(dscores, queries, NN_DIMS))

        if j == CHUNKS - 1:
            gkbuf[...] = (dk[...] * SCALE).astype(jnp.bfloat16)
            gvbuf[...] = dv[...].astype(jnp.bfloat16)

        for step in ORDER:
            s, h, device = peer(step)
            start_remote(out_copies(j, s, h), device)
            if j == CHUNKS - 1:
                start_remote(kv_copies(s, h), device)

        start_local(out_copies(j, low, c))
        if j == CHUNKS - 1:
            start_local(kv_copies(low, c))

    sent = pl.ds(0, LENGTH - ROWS // 2)
    for j in range(CHUNKS):
        for buf, sem in (
            (qbuf[j], send_q), (gbuf[j], send_g), (abuf.at[j], send_a), (gqbuf.at[j], send_gq)
        ):
            part = buf.at[:, sent, :]
            pltpu.make_async_copy(part, part, sem.at[j]).wait()
    for buf, sem in (
        (kbuf, send_kv.at[0]), (vbuf, send_kv.at[1]), (gkbuf, send_gkv.at[0]), (gvbuf, send_gkv.at[1])
    ):
        part = buf.at[:, sent, :]
        pltpu.make_async_copy(part, part, sem).wait()
    for n, ref in enumerate((attn_out, gq_out, gk_out, gv_out)):
        pltpu.make_async_copy(ref, ref, recv_out.at[n]).wait()


def shards(query_proj, key_proj, value_proj, grad_attn, doc_lengths, mask_tiles, pair_flags):
    bf16, f32 = jnp.bfloat16, jnp.float32
    dma = pltpu.SemaphoreType.DMA
    anywhere = pl.BlockSpec(memory_space=pl.ANY)
    scalars = pl.BlockSpec(memory_space=pltpu.SMEM)
    wide = pltpu.VMEM((CHUNKS, 2, LENGTH, WIDTH), bf16)
    chunk = pltpu.VMEM((2, LENGTH, WIDTH), bf16)
    thin = pltpu.VMEM((2, LENGTH, HEAD), bf16)
    total = pltpu.VMEM((2, LENGTH, HEAD), f32)
    return finish(pl.pallas_call(
        kernel,
        out_shape=tuple(
            jax.ShapeDtypeStruct(a.shape, bf16)
            for a in (query_proj, query_proj, key_proj, value_proj)
        ),
        in_specs=[anywhere] * 4 + [scalars] * 3,
        out_specs=(anywhere,) * 4,
        scratch_shapes=[
            thin, thin, wide, wide, total, total, thin, thin,
            pltpu.VMEM((2, BIAS_ROWS, BLOCK), f32),
            dma((CHUNKS,)), dma((CHUNKS,)), dma((2,)),
            dma((CHUNKS,)), dma((CHUNKS,)), dma((2,)),
            dma((4,)), dma((CHUNKS,)), dma((CHUNKS,)), dma((2,)),
            *[chunk] * (2 * CHUNKS),
        ],
        compiler_params=pltpu.CompilerParams(
            collective_id=0, has_side_effects=True, vmem_limit_bytes=48 * 2**20
        ),
    )(*[
        pltpu.with_memory_space_constraint(x, pltpu.HBM)
        for x in (
            query_proj, key_proj, value_proj, grad_attn,
            doc_lengths.T, jnp.transpose(mask_tiles, (1, 2, 0)), pair_flags,
        )
    ]))


def finish_kernel(*refs):
    ins, outs, sem = refs[:4], refs[4:8], refs[8]
    for n in range(4):
        pltpu.make_async_copy(ins[n], outs[n], sem.at[n]).start()
    for n in range(4):
        pltpu.make_async_copy(ins[n], outs[n], sem.at[n]).wait()


def finish(arrays):
    anywhere = pl.BlockSpec(memory_space=pl.ANY)
    return pl.pallas_call(
        finish_kernel,
        out_shape=tuple(jax.ShapeDtypeStruct(a.shape, a.dtype) for a in arrays),
        in_specs=[anywhere] * 4,
        out_specs=(anywhere,) * 4,
        scratch_shapes=[pltpu.SemaphoreType.DMA((4,))],
    )(*[pltpu.with_memory_space_constraint(x, pltpu.VMEM) for x in arrays])


def solution(mesh):
    split = P("dp", "ctx", None)
    return jax.shard_map(
        shards,
        mesh=mesh,
        in_specs=(split,) * 4 + (P(),) * 3,
        out_specs=(split,) * 4,
        check_vma=False,
    )
```

```python
import functools
import math

import jax
import jax.numpy as jnp
from jax import lax
from jax.experimental import pallas as pl
from jax.experimental.pallas import tpu as pltpu
from jax.sharding import PartitionSpec as P

MESH = pl.DeviceIdType.MESH
HEAD = 128
RATIO = 4
CTX = 8
ROWS = 64
LENGTH = 512
BLOCK = 128
CHUNKS = 4
HEADS_PER_CHUNK = RATIO // CHUNKS
WIDTH = HEADS_PER_CHUNK * HEAD
PEERS = 2 * CTX
ORDER = (
    (1, 1), (3, 3), (2, 2), (0, 1), (1, 0), (3, 2), (2, 3), (0, 2),
    (3, 1), (1, 2), (2, 0), (0, 3), (1, 3), (3, 0), (2, 1),
)
SCALE = HEAD ** (-0.5)
EXP2_SCALE = SCALE / math.log(2.0)
COLUMN_BLOCKS = ((0,), (0, 1), (0, 1, 2), (0, 2, 3))
BIAS_START = (0, 128, 384, 768)
BIAS_ROWS = 1152
NT_DIMS = (((1,), (1,)), ((), ()))
TN_DIMS = (((0,), (0,)), ((), ()))
NN_DIMS = (((1,), (0,)), ((), ()))


def mm(a, b, dims):
    return lax.dot_general(a, b, dims, preferred_element_type=jnp.float32)


def take_columns(ref, slot, b):
    blocks = COLUMN_BLOCKS[b]
    if blocks == tuple(range(len(blocks))):
        return ref[slot, 0 : BLOCK * len(blocks), :]
    return jnp.concatenate(
        [ref[slot, BLOCK * cb : BLOCK * (cb + 1), :] for cb in blocks], axis=0
    )


def kernel(
    q_in, k_in, v_in, g_in, lengths, tiles, flags,
    attn_out, gq_out, gk_out, gv_out,
    kbuf, vbuf, abuf, gqbuf, dk, dv, gkbuf, gvbuf, bias,
    recv_q, recv_g, recv_kv, send_q, send_g, send_kv,
    recv_out, send_a, send_gq, send_gkv,
    *chunk_bufs,
):
    qbuf, gbuf = chunk_bufs[:CHUNKS], chunk_bufs[CHUNKS:]
    dp = lax.axis_index("dp")
    c = lax.axis_index("ctx")
    half = lax.axis_size("dp") // 2
    low = dp // half
    zc = dp % half

    def peer(step):
        dx, dy = step
        s = (low + dy % 2) % 2
        h = (c // 4 + dy // 2) % 2 * 4 + (c % 4 + dx) % 4
        return s, h, {"dp": s * half + zc, "ctx": h}

    barrier = pltpu.get_barrier_semaphore()

    for step in ORDER:
        _, _, device = peer(step)
        pl.semaphore_signal(barrier, inc=1, device_id=device, device_id_type=MESH)

    pl.semaphore_wait(barrier, PEERS - 1)

    my_rows = pl.ds(pl.multiple_of(c * ROWS, ROWS), ROWS)

    def in_copies(j, s, h):
        wide = pl.ds(pl.multiple_of(h * (RATIO * HEAD) + j * WIDTH, WIDTH), WIDTH)
        out = [
            (q_in.at[s, :, wide], qbuf[j].at[low, my_rows, :], send_q.at[j], recv_q.at[j]),
            (g_in.at[s, :, wide], gbuf[j].at[low, my_rows, :], send_g.at[j], recv_g.at[j]),
        ]
        if j == 0:
            thin = pl.ds(pl.multiple_of(h * HEAD, HEAD), HEAD)
            out = [
                (k_in.at[s, :, thin], kbuf.at[low, my_rows, :], send_kv.at[0], recv_kv.at[0]),
                (v_in.at[s, :, thin], vbuf.at[low, my_rows, :], send_kv.at[1], recv_kv.at[1]),
            ] + out
        return out

    def start_remote(copies, device):
        for src, dst, send, recv in copies:
            pltpu.make_async_remote_copy(
                src_ref=src, dst_ref=dst, send_sem=send, recv_sem=recv,
                device_id=device, device_id_type=MESH,
            ).start()

    def start_local(copies):
        for src, dst, _, recv in copies:
            pltpu.make_async_copy(src, dst, recv).start()

    for j in range(CHUNKS):
        for step in ORDER:
            s, h, device = peer(step)
            start_remote(in_copies(j, s, h), device)

        start_local(in_copies(j, low, c))

    flag = jnp.where(flags[dp] == 1, 1, 0) * low
    lane = lax.broadcasted_iota(jnp.int32, (BLOCK, BLOCK), 1)
    sub = lax.broadcasted_iota(jnp.int32, (BLOCK, BLOCK), 0)

    def source(slot):
        return slot + flag - 2 * slot * flag

    @pl.loop(0, 2)
    def _(slot):
        seq = 2 * (source(slot) * half + zc) + low
        ends = []
        total = lengths[0, seq]
        for d in range(1, 8):
            ends.append(total)
            total = total + lengths[d, seq]
        for b in range(4):
            row = lane + BLOCK * b
            row_doc = sum((row >= e).astype(jnp.int32) for e in ends)
            for n, cb in enumerate(COLUMN_BLOCKS[b]):
                col = sub + BLOCK * cb
                col_doc = sum((col >= e).astype(jnp.int32) for e in ends)
                first = jnp.where(lane < 64, tiles[2 * b, 2 * cb, seq], tiles[2 * b + 1, 2 * cb, seq])
                second = jnp.where(
                    lane < 64, tiles[2 * b, 2 * cb + 1, seq], tiles[2 * b + 1, 2 * cb + 1, seq]
                )
                tile = jnp.where(sub < 64, first, second)
                allowed = (col <= row) & ((col_doc == row_doc) | (col_doc == 0)) & (tile == 1)
                at = BIAS_START[b] + BLOCK * n
                bias[slot, at : at + BLOCK, :] = jnp.where(allowed, 0.0, -1e30)

    dk[...] = jnp.zeros_like(dk)
    dv[...] = jnp.zeros_like(dv)

    pltpu.make_async_copy(kbuf, kbuf, recv_kv.at[0]).wait()
    pltpu.make_async_copy(vbuf, vbuf, recv_kv.at[1]).wait()

    def add_columns(ref, slot, b, value):
        for n, cb in enumerate(COLUMN_BLOCKS[b]):
            ref[slot, BLOCK * cb : BLOCK * (cb + 1), :] += value[BLOCK * n : BLOCK * (n + 1)]

    def out_copies(j, s, h):
        rows = pl.ds(pl.multiple_of(h * ROWS, ROWS), ROWS)
        wide = pl.ds(pl.multiple_of(c * (RATIO * HEAD) + j * WIDTH, WIDTH), WIDTH)
        return [
            (abuf.at[j, s, rows, :], attn_out.at[low, :, wide], send_a.at[j], recv_out.at[0]),
            (gqbuf.at[j, s, rows, :], gq_out.at[low, :, wide], send_gq.at[j], recv_out.at[1]),
        ]

    def kv_copies(s, h):
        rows = pl.ds(pl.multiple_of(h * ROWS, ROWS), ROWS)
        thin = pl.ds(pl.multiple_of(c * HEAD, HEAD), HEAD)
        return [
            (gkbuf.at[s, rows, :], gk_out.at[low, :, thin], send_gkv.at[0], recv_out.at[2]),
            (gvbuf.at[s, rows, :], gv_out.at[low, :, thin], send_gkv.at[1], recv_out.at[3]),
        ]

    for j in range(CHUNKS):
        pltpu.make_async_copy(qbuf[j], qbuf[j], recv_q.at[j]).wait()
        pltpu.make_async_copy(gbuf[j], gbuf[j], recv_g.at[j]).wait()

        @pl.loop(0, 2)
        def _(slot, j=j):
            u = source(slot)
            for b in range(4):
                rows = slice(BLOCK * b, BLOCK * (b + 1))
                n_cols = BLOCK * len(COLUMN_BLOCKS[b])
                keys = take_columns(kbuf, u, b)
                values = take_columns(vbuf, u, b)
                heads = [slice(HEAD * h, HEAD * (h + 1)) for h in range(HEADS_PER_CHUNK)]
                queries = jnp.concatenate([qbuf[j][u, rows, h] for h in heads], axis=0)
                grads = jnp.concatenate([gbuf[j][u, rows, h] for h in heads], axis=0)
                mask = bias[slot, BIAS_START[b] : BIAS_START[b] + n_cols, :]
                mask = jnp.concatenate([mask] * HEADS_PER_CHUNK, axis=1)
                scores = mm(keys, queries, NT_DIMS) + mask
                peak = jnp.max(scores, axis=0, keepdims=True)
                expd = jnp.exp2((scores - peak) * EXP2_SCALE)
                probs = expd * (1.0 / jnp.sum(expd, axis=0, keepdims=True))
                probs_b = probs.astype(jnp.bfloat16)
                dprobs = mm(values, grads, NT_DIMS)
                delta = jnp.sum(probs * dprobs, axis=0, keepdims=True)
                dscores = (probs * (dprobs - delta)).astype(jnp.bfloat16)
                attn = mm(probs_b, values, TN_DIMS).astype(jnp.bfloat16)
                gq = (mm(dscores, keys, TN_DIMS) * SCALE).astype(jnp.bfloat16)
                for n, h in enumerate(heads):
                    abuf[j, slot, rows, h] = attn[BLOCK * n : BLOCK * (n + 1)]
                    gqbuf[j, slot, rows, h] = gq[BLOCK * n : BLOCK * (n + 1)]
                add_columns(dv, slot, b, mm(probs_b, grads, NN_DIMS))
                add_columns(dk, slot, b, mm(dscores, queries, NN_DIMS))

        if j == CHUNKS - 1:
            gkbuf[...] = (dk[...] * SCALE).astype(jnp.bfloat16)
            gvbuf[...] = dv[...].astype(jnp.bfloat16)

        for step in ORDER:
            s, h, device = peer(step)
            start_remote(out_copies(j, s, h), device)
            if j == CHUNKS - 1:
                start_remote(kv_copies(s, h), device)

        start_local(out_copies(j, low, c))
        if j == CHUNKS - 1:
            start_local(kv_copies(low, c))

    sent = pl.ds(0, LENGTH - ROWS // 2)
    for j in range(CHUNKS):
        for buf, sem in (
            (qbuf[j], send_q), (gbuf[j], send_g), (abuf.at[j], send_a), (gqbuf.at[j], send_gq)
        ):
            part = buf.at[:, sent, :]
            pltpu.make_async_copy(part, part, sem.at[j]).wait()
    for buf, sem in (
        (kbuf, send_kv.at[0]), (vbuf, send_kv.at[1]), (gkbuf, send_gkv.at[0]), (gvbuf, send_gkv.at[1])
    ):
        part = buf.at[:, sent, :]
        pltpu.make_async_copy(part, part, sem).wait()
    for n, ref in enumerate((attn_out, gq_out, gk_out, gv_out)):
        pltpu.make_async_copy(ref, ref, recv_out.at[n]).wait()


def shards(query_proj, key_proj, value_proj, grad_attn, doc_lengths, mask_tiles, pair_flags):
    bf16, f32 = jnp.bfloat16, jnp.float32
    dma = pltpu.SemaphoreType.DMA
    anywhere = pl.BlockSpec(memory_space=pl.ANY)
    scalars = pl.BlockSpec(memory_space=pltpu.SMEM)
    wide = pltpu.VMEM((CHUNKS, 2, LENGTH, WIDTH), bf16)
    chunk = pltpu.VMEM((2, LENGTH, WIDTH), bf16)
    thin = pltpu.VMEM((2, LENGTH, HEAD), bf16)
    total = pltpu.VMEM((2, LENGTH, HEAD), f32)
    return finish(pl.pallas_call(
        kernel,
        out_shape=tuple(
            jax.ShapeDtypeStruct(a.shape, bf16)
            for a in (query_proj, query_proj, key_proj, value_proj)
        ),
        in_specs=[anywhere] * 4 + [scalars] * 3,
        out_specs=(anywhere,) * 4,
        scratch_shapes=[
            thin, thin, wide, wide, total, total, thin, thin,
            pltpu.VMEM((2, BIAS_ROWS, BLOCK), f32),
            dma((CHUNKS,)), dma((CHUNKS,)), dma((2,)),
            dma((CHUNKS,)), dma((CHUNKS,)), dma((2,)),
            dma((4,)), dma((CHUNKS,)), dma((CHUNKS,)), dma((2,)),
            *[chunk] * (2 * CHUNKS),
        ],
        compiler_params=pltpu.CompilerParams(
            collective_id=0, has_side_effects=True, vmem_limit_bytes=48 * 2**20
        ),
    )(*[
        pltpu.with_memory_space_constraint(x, pltpu.HBM)
        for x in (
            query_proj, key_proj, value_proj, grad_attn,
            doc_lengths.T, jnp.transpose(mask_tiles, (1, 2, 0)), pair_flags,
        )
    ]))


def finish_kernel(*refs):
    ins, outs, sem = refs[:4], refs[4:8], refs[8]
    for n in range(4):
        pltpu.make_async_copy(ins[n], outs[n], sem.at[n]).start()
    for n in range(4):
        pltpu.make_async_copy(ins[n], outs[n], sem.at[n]).wait()


def finish(arrays):
    anywhere = pl.BlockSpec(memory_space=pl.ANY)
    return pl.pallas_call(
        finish_kernel,
        out_shape=tuple(jax.ShapeDtypeStruct(a.shape, a.dtype) for a in arrays),
        in_specs=[anywhere] * 4,
        out_specs=(anywhere,) * 4,
        scratch_shapes=[pltpu.SemaphoreType.DMA((4,))],
    )(*[pltpu.with_memory_space_constraint(x, pltpu.VMEM) for x in arrays])


def solution(mesh):
    split = P("dp", "ctx", None)
    return jax.shard_map(
        shards,
        mesh=mesh,
        in_specs=(split,) * 4 + (P(),) * 3,
        out_specs=(split,) * 4,
        check_vma=False,
    )
```

```python
import functools
import math

import jax
import jax.numpy as jnp
from jax import lax
from jax.experimental import pallas as pl
from jax.experimental.pallas import tpu as pltpu
from jax.sharding import PartitionSpec as P

MESH = pl.DeviceIdType.MESH
HEAD = 128
RATIO = 4
CTX = 8
ROWS = 64
LENGTH = 512
BLOCK = 128
CHUNKS = 4
HEADS_PER_CHUNK = RATIO // CHUNKS
WIDTH = HEADS_PER_CHUNK * HEAD
PEERS = 2 * CTX
ORDER = (
    (1, 1), (3, 3), (2, 2), (0, 1), (1, 0), (3, 2), (2, 3), (0, 2),
    (3, 1), (1, 2), (2, 0), (0, 3), (1, 3), (3, 0), (2, 1),
)
SCALE = HEAD ** (-0.5)
EXP2_SCALE = SCALE / math.log(2.0)
COLUMN_BLOCKS = ((0,), (0, 1), (0, 1, 2), (0, 2, 3))
BIAS_START = (0, 128, 384, 768)
BIAS_ROWS = 1152
NT_DIMS = (((1,), (1,)), ((), ()))
TN_DIMS = (((0,), (0,)), ((), ()))
NN_DIMS = (((1,), (0,)), ((), ()))


def mm(a, b, dims):
    return lax.dot_general(a, b, dims, preferred_element_type=jnp.float32)


def take_columns(ref, slot, b):
    blocks = COLUMN_BLOCKS[b]
    if blocks == tuple(range(len(blocks))):
        return ref[slot, 0 : BLOCK * len(blocks), :]
    return jnp.concatenate(
        [ref[slot, BLOCK * cb : BLOCK * (cb + 1), :] for cb in blocks], axis=0
    )


def kernel(
    q_in, k_in, v_in, g_in, lengths_in, tiles_in, flags_in,
    attn_out, gq_out, gk_out, gv_out,
    kbuf, vbuf, abuf, gqbuf, dk, dv, gkbuf, gvbuf, bias,
    recv_q, recv_g, recv_kv, send_q, send_g, send_kv,
    recv_out, send_a, send_gq, send_gkv,
    lengths, tiles, flags, scalar_sem,
    *chunk_bufs,
):
    qbuf, gbuf = chunk_bufs[:CHUNKS], chunk_bufs[CHUNKS:]
    dp = lax.axis_index("dp")
    c = lax.axis_index("ctx")
    half = lax.axis_size("dp") // 2
    low = dp // half
    zc = dp % half

    def peer(step):
        dx, dy = step
        s = (low + dy % 2) % 2
        h = (c // 4 + dy // 2) % 2 * 4 + (c % 4 + dx) % 4
        return s, h, {"dp": s * half + zc, "ctx": h}

    scalar_copies = [
        pltpu.make_async_copy(src, dst, scalar_sem.at[n])
        for n, (src, dst) in enumerate(((lengths_in, lengths), (tiles_in, tiles), (flags_in, flags)))
    ]
    for copy in scalar_copies:
        copy.start()

    barrier = pltpu.get_barrier_semaphore()

    for step in ORDER:
        _, _, device = peer(step)
        pl.semaphore_signal(barrier, inc=1, device_id=device, device_id_type=MESH)

    pl.semaphore_wait(barrier, PEERS - 1)

    my_rows = pl.ds(pl.multiple_of(c * ROWS, ROWS), ROWS)

    def in_copies(j, s, h):
        wide = pl.ds(pl.multiple_of(h * (RATIO * HEAD) + j * WIDTH, WIDTH), WIDTH)
        out = [
            (q_in.at[s, :, wide], qbuf[j].at[low, my_rows, :], send_q.at[j], recv_q.at[j]),
            (g_in.at[s, :, wide], gbuf[j].at[low, my_rows, :], send_g.at[j], recv_g.at[j]),
        ]
        if j == 0:
            thin = pl.ds(pl.multiple_of(h * HEAD, HEAD), HEAD)
            out = [
                (k_in.at[s, :, thin], kbuf.at[low, my_rows, :], send_kv.at[0], recv_kv.at[0]),
                (v_in.at[s, :, thin], vbuf.at[low, my_rows, :], send_kv.at[1], recv_kv.at[1]),
            ] + out
        return out

    def start_remote(copies, device):
        for src, dst, send, recv in copies:
            pltpu.make_async_remote_copy(
                src_ref=src, dst_ref=dst, send_sem=send, recv_sem=recv,
                device_id=device, device_id_type=MESH,
            ).start()

    def start_local(copies):
        for src, dst, _, recv in copies:
            pltpu.make_async_copy(src, dst, recv).start()

    for j in range(CHUNKS):
        for step in ORDER:
            s, h, device = peer(step)
            start_remote(in_copies(j, s, h), device)

        start_local(in_copies(j, low, c))

    for copy in scalar_copies:
        copy.wait()
    flag = jnp.where(flags[dp] == 1, 1, 0) * low
    lane = lax.broadcasted_iota(jnp.int32, (BLOCK, BLOCK), 1)
    sub = lax.broadcasted_iota(jnp.int32, (BLOCK, BLOCK), 0)

    def source(slot):
        return slot + flag - 2 * slot * flag

    @pl.loop(0, 2)
    def _(slot):
        seq = 2 * (source(slot) * half + zc) + low
        ends = []
        total = lengths[0, seq]
        for d in range(1, 8):
            ends.append(total)
            total = total + lengths[d, seq]
        for b in range(4):
            row = lane + BLOCK * b
            row_doc = sum((row >= e).astype(jnp.int32) for e in ends)
            for n, cb in enumerate(COLUMN_BLOCKS[b]):
                col = sub + BLOCK * cb
                col_doc = sum((col >= e).astype(jnp.int32) for e in ends)
                first = jnp.where(lane < 64, tiles[2 * b, 2 * cb, seq], tiles[2 * b + 1, 2 * cb, seq])
                second = jnp.where(
                    lane < 64, tiles[2 * b, 2 * cb + 1, seq], tiles[2 * b + 1, 2 * cb + 1, seq]
                )
                tile = jnp.where(sub < 64, first, second)
                allowed = (col <= row) & ((col_doc == row_doc) | (col_doc == 0)) & (tile == 1)
                at = BIAS_START[b] + BLOCK * n
                bias[slot, at : at + BLOCK, :] = jnp.where(allowed, 0.0, -1e30)

    dk[...] = jnp.zeros_like(dk)
    dv[...] = jnp.zeros_like(dv)

    pltpu.make_async_copy(kbuf, kbuf, recv_kv.at[0]).wait()
    pltpu.make_async_copy(vbuf, vbuf, recv_kv.at[1]).wait()

    def add_columns(ref, slot, b, value):
        for n, cb in enumerate(COLUMN_BLOCKS[b]):
            ref[slot, BLOCK * cb : BLOCK * (cb + 1), :] += value[BLOCK * n : BLOCK * (n + 1)]

    def out_copies(j, s, h):
        rows = pl.ds(pl.multiple_of(h * ROWS, ROWS), ROWS)
        wide = pl.ds(pl.multiple_of(c * (RATIO * HEAD) + j * WIDTH, WIDTH), WIDTH)
        return [
            (abuf.at[j, s, rows, :], attn_out.at[low, :, wide], send_a.at[j], recv_out.at[0]),
            (gqbuf.at[j, s, rows, :], gq_out.at[low, :, wide], send_gq.at[j], recv_out.at[1]),
        ]

    def kv_copies(s, h):
        rows = pl.ds(pl.multiple_of(h * ROWS, ROWS), ROWS)
        thin = pl.ds(pl.multiple_of(c * HEAD, HEAD), HEAD)
        return [
            (gkbuf.at[s, rows, :], gk_out.at[low, :, thin], send_gkv.at[0], recv_out.at[2]),
            (gvbuf.at[s, rows, :], gv_out.at[low, :, thin], send_gkv.at[1], recv_out.at[3]),
        ]

    for j in range(CHUNKS):
        pltpu.make_async_copy(qbuf[j], qbuf[j], recv_q.at[j]).wait()
        pltpu.make_async_copy(gbuf[j], gbuf[j], recv_g.at[j]).wait()

        @pl.loop(0, 2)
        def _(slot, j=j):
            u = source(slot)
            for b in range(4):
                rows = slice(BLOCK * b, BLOCK * (b + 1))
                n_cols = BLOCK * len(COLUMN_BLOCKS[b])
                keys = take_columns(kbuf, u, b)
                values = take_columns(vbuf, u, b)
                heads = [slice(HEAD * h, HEAD * (h + 1)) for h in range(HEADS_PER_CHUNK)]
                queries = jnp.concatenate([qbuf[j][u, rows, h] for h in heads], axis=0)
                grads = jnp.concatenate([gbuf[j][u, rows, h] for h in heads], axis=0)
                mask = bias[slot, BIAS_START[b] : BIAS_START[b] + n_cols, :]
                mask = jnp.concatenate([mask] * HEADS_PER_CHUNK, axis=1)
                scores = mm(keys, queries, NT_DIMS) + mask
                peak = jnp.max(scores, axis=0, keepdims=True)
                expd = jnp.exp2((scores - peak) * EXP2_SCALE)
                probs = expd * (1.0 / jnp.sum(expd, axis=0, keepdims=True))
                probs_b = probs.astype(jnp.bfloat16)
                dprobs = mm(values, grads, NT_DIMS)
                delta = jnp.sum(probs * dprobs, axis=0, keepdims=True)
                dscores = (probs * (dprobs - delta)).astype(jnp.bfloat16)
                attn = mm(probs_b, values, TN_DIMS).astype(jnp.bfloat16)
                gq = (mm(dscores, keys, TN_DIMS) * SCALE).astype(jnp.bfloat16)
                for n, h in enumerate(heads):
                    abuf[j, slot, rows, h] = attn[BLOCK * n : BLOCK * (n + 1)]
                    gqbuf[j, slot, rows, h] = gq[BLOCK * n : BLOCK * (n + 1)]
                add_columns(dv, slot, b, mm(probs_b, grads, NN_DIMS))
                add_columns(dk, slot, b, mm(dscores, queries, NN_DIMS))

        if j == CHUNKS - 1:
            gkbuf[...] = (dk[...] * SCALE).astype(jnp.bfloat16)
            gvbuf[...] = dv[...].astype(jnp.bfloat16)

        for step in ORDER:
            s, h, device = peer(step)
            start_remote(out_copies(j, s, h), device)
            if j == CHUNKS - 1:
                start_remote(kv_copies(s, h), device)

        start_local(out_copies(j, low, c))
        if j == CHUNKS - 1:
            start_local(kv_copies(low, c))

    sent = pl.ds(0, LENGTH - ROWS // 2)
    for j in range(CHUNKS):
        for buf, sem in (
            (qbuf[j], send_q), (gbuf[j], send_g), (abuf.at[j], send_a), (gqbuf.at[j], send_gq)
        ):
            part = buf.at[:, sent, :]
            pltpu.make_async_copy(part, part, sem.at[j]).wait()
    for buf, sem in (
        (kbuf, send_kv.at[0]), (vbuf, send_kv.at[1]), (gkbuf, send_gkv.at[0]), (gvbuf, send_gkv.at[1])
    ):
        part = buf.at[:, sent, :]
        pltpu.make_async_copy(part, part, sem).wait()
    for n, ref in enumerate((attn_out, gq_out, gk_out, gv_out)):
        pltpu.make_async_copy(ref, ref, recv_out.at[n]).wait()


def shards(query_proj, key_proj, value_proj, grad_attn, doc_lengths, mask_tiles, pair_flags):
    bf16, f32 = jnp.bfloat16, jnp.float32
    dma = pltpu.SemaphoreType.DMA
    anywhere = pl.BlockSpec(memory_space=pl.ANY)
    scalars = (doc_lengths.T, jnp.transpose(mask_tiles, (1, 2, 0)), pair_flags)
    wide = pltpu.VMEM((CHUNKS, 2, LENGTH, WIDTH), bf16)
    chunk = pltpu.VMEM((2, LENGTH, WIDTH), bf16)
    thin = pltpu.VMEM((2, LENGTH, HEAD), bf16)
    total = pltpu.VMEM((2, LENGTH, HEAD), f32)
    return finish(pl.pallas_call(
        kernel,
        out_shape=tuple(
            jax.ShapeDtypeStruct(a.shape, bf16)
            for a in (query_proj, query_proj, key_proj, value_proj)
        ),
        in_specs=[anywhere] * 7,
        out_specs=(anywhere,) * 4,
        scratch_shapes=[
            thin, thin, wide, wide, total, total, thin, thin,
            pltpu.VMEM((2, BIAS_ROWS, BLOCK), f32),
            dma((CHUNKS,)), dma((CHUNKS,)), dma((2,)),
            dma((CHUNKS,)), dma((CHUNKS,)), dma((2,)),
            dma((4,)), dma((CHUNKS,)), dma((CHUNKS,)), dma((2,)),
            *[pltpu.SMEM(a.shape, a.dtype) for a in scalars], dma((3,)),
            *[chunk] * (2 * CHUNKS),
        ],
        compiler_params=pltpu.CompilerParams(
            collective_id=0, has_side_effects=True, vmem_limit_bytes=48 * 2**20
        ),
    )(*[
        pltpu.with_memory_space_constraint(x, pltpu.HBM)
        for x in (query_proj, key_proj, value_proj, grad_attn, *scalars)
    ]))


def finish_kernel(*refs):
    ins, outs, sem = refs[:4], refs[4:8], refs[8]
    for n in range(4):
        pltpu.make_async_copy(ins[n], outs[n], sem.at[n]).start()
    for n in range(4):
        pltpu.make_async_copy(ins[n], outs[n], sem.at[n]).wait()


def finish(arrays):
    anywhere = pl.BlockSpec(memory_space=pl.ANY)
    return pl.pallas_call(
        finish_kernel,
        out_shape=tuple(jax.ShapeDtypeStruct(a.shape, a.dtype) for a in arrays),
        in_specs=[anywhere] * 4,
        out_specs=(anywhere,) * 4,
        scratch_shapes=[pltpu.SemaphoreType.DMA((4,))],
    )(*[pltpu.with_memory_space_constraint(x, pltpu.VMEM) for x in arrays])


def solution(mesh):
    split = P("dp", "ctx", None)
    return jax.shard_map(
        shards,
        mesh=mesh,
        in_specs=(split,) * 4 + (P(),) * 3,
        out_specs=(split,) * 4,
        check_vma=False,
    )
```

```python
import functools
import math

import jax
import jax.numpy as jnp
from jax import lax
from jax.experimental import pallas as pl
from jax.experimental.pallas import tpu as pltpu
from jax.sharding import PartitionSpec as P

MESH = pl.DeviceIdType.MESH
HEAD = 128
RATIO = 4
ROWS = 64
LENGTH = 512
BLOCK = 128
SIDE = 4
PAIR = 2 * HEAD
QPAIR = RATIO * PAIR
E_CHUNKS = 4
E_WIDTH = QPAIR // E_CHUNKS
O_CHUNKS = 2
O_WIDTH = QPAIR // O_CHUNKS
SCALE = HEAD ** (-0.5)
EXP2_SCALE = SCALE / math.log(2.0)
COLUMN_BLOCKS = ((0,), (0, 1), (0, 1, 2), (0, 2, 3))
BIAS_START = (0, 128, 0, 384)
NT_DIMS = (((1,), (1,)), ((), ()))
TN_DIMS = (((0,), (0,)), ((), ()))
NN_DIMS = (((1,), (0,)), ((), ()))
STEPS = (1, 3, 2)


def mm(a, b, dims):
    return lax.dot_general(a, b, dims, preferred_element_type=jnp.float32)


def attend(queries, grads, keys, values, mask):
    scores = mm(keys, queries, NT_DIMS) + mask
    peak = jnp.max(scores, axis=0, keepdims=True)
    expd = jnp.exp2((scores - peak) * EXP2_SCALE)
    probs = expd * (1.0 / jnp.sum(expd, axis=0, keepdims=True))
    probs_b = probs.astype(jnp.bfloat16)
    dprobs = mm(values, grads, NT_DIMS)
    delta = jnp.sum(probs * dprobs, axis=0, keepdims=True)
    dscores = (probs * (dprobs - delta)).astype(jnp.bfloat16)
    attn = mm(probs_b, values, TN_DIMS).astype(jnp.bfloat16)
    gq = (mm(dscores, keys, TN_DIMS) * SCALE).astype(jnp.bfloat16)
    return attn, gq, mm(dscores, queries, NN_DIMS), mm(probs_b, grads, NN_DIMS)


def kernel(
    q_in, k_in, v_in, g_in, lengths_in, tiles_in, flags_in,
    attn_out, gq_out, gk_out, gv_out,
    ek, ev, ok, ov, ea, egq, oa, ogq, edk, edv, odk, odv, ebias, obias,
    esk, esv, erk, erv, egk, egv, opk, opv, rpk, rpv, ogk, ogv,
    lengths, tiles, flags, scalar_sem,
    r_eq, r_eg, r_oq, r_og, r_kv, r_all, r_fwd, r_ep, r_rs, r_out,
    s_eq, s_eg, s_oq, s_og, s_kv, s_all, s_fwd, s_ep, s_rs,
    s_ea, s_egq, s_oa, s_ogq, s_gkv,
    *bufs,
):
    eq, eg = bufs[0:E_CHUNKS], bufs[E_CHUNKS : 2 * E_CHUNKS]
    oq, og = bufs[2 * E_CHUNKS : 2 * E_CHUNKS + O_CHUNKS], bufs[2 * E_CHUNKS + O_CHUNKS :]
    dp = lax.axis_index("dp")
    c = lax.axis_index("ctx")
    half = lax.axis_size("dp") // 2
    low = dp // half
    zc = dp % half
    hi = c // SIDE
    x = c % SIDE
    y = 2 * hi + low

    def along_x(step):
        xn = (x + step) % SIDE
        return xn, {"dp": dp, "ctx": hi * SIDE + xn}

    def along_y(step):
        yn = (y + step) % SIDE
        return yn, {"dp": (yn % 2) * half + zc, "ctx": (yn // 2) * SIDE + x}

    def across(device_hi):
        return {"dp": dp, "ctx": device_hi * SIDE + x}

    scalar_copies = [
        pltpu.make_async_copy(src, dst, scalar_sem.at[n])
        for n, (src, dst) in enumerate(((lengths_in, lengths), (tiles_in, tiles), (flags_in, flags)))
    ]
    for copy in scalar_copies:
        copy.start()

    barrier = pltpu.get_barrier_semaphore()
    for step in STEPS:
        for along in (along_x, along_y):
            pl.semaphore_signal(barrier, inc=1, device_id=along(step)[1], device_id_type=MESH)
    pl.semaphore_wait(barrier, 6)

    def send(src, dst, send_sem, recv_sem, device):
        pltpu.make_async_remote_copy(
            src_ref=src, dst_ref=dst, send_sem=send_sem, recv_sem=recv_sem,
            device_id=device, device_id_type=MESH,
        ).start()

    def keep(src, dst, _, recv_sem):
        pltpu.make_async_copy(src, dst, recv_sem).start()

    def wait(ref, sem):
        pltpu.make_async_copy(ref, ref, sem).wait()

    def at(start, size):
        return pl.ds(pl.multiple_of(start, size), size)

    rows_c = at(c * ROWS, ROWS)
    rows_x = at(x * ROWS, ROWS)
    rows_hi = at(hi * ROWS, ROWS)

    def kv_even(n):
        cols = at(n * PAIR, PAIR)
        return [
            (k_in.at[0, :, cols], ek.at[rows_c, :], s_kv.at[0], r_kv.at[0]),
            (v_in.at[0, :, cols], ev.at[rows_c, :], s_kv.at[1], r_kv.at[1]),
        ]

    def kv_odd(n):
        cols = at(n * PAIR, PAIR)
        return [
            (k_in.at[1, :, cols], ok.at[low, rows_c, :], s_kv.at[2], r_kv.at[2]),
            (v_in.at[1, :, cols], ov.at[low, rows_c, :], s_kv.at[3], r_kv.at[3]),
        ]

    def q_even(n, j):
        cols = at(n * QPAIR + j * E_WIDTH, E_WIDTH)
        return [
            (q_in.at[0, :, cols], eq[j].at[rows_x, :], s_eq.at[j], r_eq.at[j]),
            (g_in.at[0, :, cols], eg[j].at[rows_x, :], s_eg.at[j], r_eg.at[j]),
        ]

    def q_odd(n, j):
        cols = at(n * QPAIR + j * O_WIDTH, O_WIDTH)
        return [
            (q_in.at[1, :, cols], oq[j].at[low, rows_hi, :], s_oq.at[j], r_oq.at[j]),
            (g_in.at[1, :, cols], og[j].at[low, rows_hi, :], s_og.at[j], r_og.at[j]),
        ]

    def exchange(even=None, odd=None):
        for step in STEPS:
            if odd is not None:
                n, device = along_y(step)
                for item in odd(n):
                    send(*item, device)
            if even is not None:
                n, device = along_x(step)
                for item in even(n):
                    send(*item, device)
        for item in (odd(y) if odd is not None else []) + (even(x) if even is not None else []):
            keep(*item)

    exchange(kv_even, kv_odd)
    exchange(lambda n: q_even(n, 0), lambda n: q_odd(n, 0))

    for copy in scalar_copies:
        copy.wait()
    flag = jnp.where(flags[dp] == 1, 1, 0)
    lane = lax.broadcasted_iota(jnp.int32, (BLOCK, BLOCK), 1)
    sub = lax.broadcasted_iota(jnp.int32, (BLOCK, BLOCK), 0)

    def segment_ends(seq):
        ends = []
        total = lengths[0, seq]
        for d in range(1, 8):
            ends.append(total)
            total = total + lengths[d, seq]
        return ends

    def addend(ends, row, col, tile):
        row_doc = sum((row >= e).astype(jnp.int32) for e in ends)
        col_doc = sum((col >= e).astype(jnp.int32) for e in ends)
        allowed = (col <= row) & ((col_doc == row_doc) | (col_doc == 0)) & (tile == 1)
        return jnp.where(allowed, 0.0, -1e30)

    wait(ok.at[:, 0 : 2 * ROWS, :], r_kv.at[2])
    wait(ov.at[:, 0 : 2 * ROWS, :], r_kv.at[3])
    for step in STEPS:
        _, device = along_x(step)
        for t in range(2):
            part = at((SIDE * t + x) * ROWS, ROWS)
            for n, ref in enumerate((ok, ov)):
                send(ref.at[:, part, :], ref.at[:, part, :], s_all.at[n], r_all.at[n], device)
    wait(ek.at[0 : SIDE * ROWS, :], r_kv.at[0])
    wait(ev.at[0 : SIDE * ROWS, :], r_kv.at[1])

    first = pl.ds(0, SIDE * ROWS)

    @pl.when(hi == 0)
    def _():
        for n, ref in enumerate((ek, ev)):
            send(ref.at[first, :], ref.at[first, :], s_fwd.at[n], r_fwd.at[n], across(1))

    for j in range(1, E_CHUNKS):
        odd = (lambda n, j=j: q_odd(n, j)) if j < O_CHUNKS else None
        exchange(lambda n, j=j: q_even(n, j), odd)

    for b in range(4):

        @pl.when(hi == b // 2)
        def _(b=b):
            seq = 2 * dp
            ends = segment_ends(seq)
            row = lane + BLOCK * b
            for n, cb in enumerate(COLUMN_BLOCKS[b]):
                top, bottom = (
                    jnp.where(
                        lane < 64,
                        tiles[2 * b, 2 * cb + m, seq],
                        tiles[2 * b + 1, 2 * cb + m, seq],
                    )
                    for m in range(2)
                )
                start = BIAS_START[b] + BLOCK * n
                ebias[start : start + BLOCK, :] = addend(
                    ends, row, sub + BLOCK * cb, jnp.where(sub < 64, top, bottom)
                )

    def source(slot):
        return slot + flag - 2 * slot * flag

    near = x + 2

    @pl.loop(0, 2)
    def _(slot):
        seq = 2 * (source(slot) * half + zc) + 1
        ends = segment_ends(seq)
        inner = lane % ROWS
        for t, start in ((0, 0), (0, BLOCK), (1, 2 * BLOCK)):
            row_tile = SIDE * t + x
            cb = start // BLOCK % 2
            tile = jnp.where(sub < 64, tiles[row_tile, 2 * cb, seq], tiles[row_tile, 2 * cb + 1, seq])
            obias[slot, start : start + BLOCK, :] = addend(
                ends, inner + row_tile * ROWS, sub + BLOCK * cb, tile
            )
        for m in range(3):
            start = 3 * BLOCK + ROWS * m
            tile = jnp.zeros_like(sub[:ROWS]) + tiles[SIDE + x, near + m, seq]
            obias[slot, start : start + ROWS, :] = addend(
                ends, inner[:ROWS] + (SIDE + x) * ROWS, sub[:ROWS] + (near + m) * ROWS, tile
            )

    for ref in (edk, edv, odk, odv):
        ref[...] = jnp.zeros_like(ref)

    def a_even(n, j):
        rows, cols = at(n * ROWS, ROWS), at(x * QPAIR + j * E_WIDTH, E_WIDTH)
        return [
            (ea.at[j, rows, :], attn_out.at[0, :, cols], s_ea.at[j], r_out.at[0]),
            (egq.at[j, rows, :], gq_out.at[0, :, cols], s_egq.at[j], r_out.at[1]),
        ]

    def a_odd(n, j):
        rows, cols = at((n // 2) * ROWS, ROWS), at(y * QPAIR + j * O_WIDTH, O_WIDTH)
        return [
            (oa.at[j, n % 2, rows, :], attn_out.at[1, :, cols], s_oa.at[j], r_out.at[0]),
            (ogq.at[j, n % 2, rows, :], gq_out.at[1, :, cols], s_ogq.at[j], r_out.at[1]),
        ]

    def kv_even_out(n):
        rows, cols = at(n * ROWS, ROWS), at(x * PAIR, PAIR)
        return [
            (egk.at[rows, :], gk_out.at[0, :, cols], s_gkv.at[0], r_out.at[2]),
            (egv.at[rows, :], gv_out.at[0, :, cols], s_gkv.at[1], r_out.at[3]),
        ]

    def kv_odd_out(n):
        cols = at(y * PAIR, PAIR)
        return [
            (ogk.at[n % 2, n // 2], gk_out.at[1, :, cols], s_gkv.at[2], r_out.at[2]),
            (ogv.at[n % 2, n // 2], gv_out.at[1, :, cols], s_gkv.at[3], r_out.at[3]),
        ]

    late = pl.ds(pl.multiple_of(near * ROWS, ROWS), 3 * ROWS)
    wait(ok.at[:, 0 : 6 * ROWS, :], r_all.at[0])
    wait(ov.at[:, 0 : 6 * ROWS, :], r_all.at[1])

    for j in range(O_CHUNKS):
        wait(oq[j], r_oq.at[j])
        wait(og[j], r_og.at[j])
        kv = slice(HEAD * j, HEAD * (j + 1))
        heads = [slice(HEAD * h, HEAD * (h + 1)) for h in range(RATIO)]

        @pl.loop(0, 2)
        def _(slot, j=j, kv=kv, heads=heads):
            u = source(slot)
            for t in range(2):
                rows = slice(ROWS * t, ROWS * (t + 1))
                queries = jnp.concatenate([oq[j][u, rows, h] for h in heads], axis=0)
                grads = jnp.concatenate([og[j][u, rows, h] for h in heads], axis=0)
                if t == 0:
                    keys, values = ok[u, 0:256, kv], ov[u, 0:256, kv]
                    mask = obias[slot, 0:256, :]
                else:
                    keys = jnp.concatenate([ok[u, 0:128, kv], ok[u, late, kv]], axis=0)
                    values = jnp.concatenate([ov[u, 0:128, kv], ov[u, late, kv]], axis=0)
                    mask = obias[slot, 256:576, :]
                attn, gq, dkp, dvp = attend(
                    queries, grads, keys, values, jnp.concatenate([mask] * 2, axis=1)
                )
                for n, h in enumerate(heads):
                    oa[j, slot, rows, h] = attn[ROWS * n : ROWS * (n + 1)]
                    ogq[j, slot, rows, h] = gq[ROWS * n : ROWS * (n + 1)]
                for ref, value in ((odk, dkp), (odv, dvp)):
                    if t == 0:
                        ref[slot, 0:256, kv] += value
                    else:
                        ref[slot, 0:128, kv] += value[:128]
                        ref[slot, late, kv] += value[128:]

        exchange(None, lambda n, j=j: a_odd(n, j))

    for t in range(8):
        rows = slice(ROWS * t, ROWS * (t + 1))
        opk[t % SIDE, :, t // SIDE] = (odk[:, rows] * SCALE).astype(jnp.bfloat16)
        opv[t % SIDE, :, t // SIDE] = odv[:, rows].astype(jnp.bfloat16)
    for step in STEPS:
        n, device = along_x(step)
        send(opk.at[n], rpk.at[step - 1], s_rs.at[0], r_rs.at[0], device)
        send(opv.at[n], rpv.at[step - 1], s_rs.at[1], r_rs.at[1], device)

    @pl.when(hi == 1)
    def _():
        wait(ek.at[first, :], r_fwd.at[0])
        wait(ev.at[first, :], r_fwd.at[1])

    for j in range(E_CHUNKS):
        wait(eq[j], r_eq.at[j])
        wait(eg[j], r_eg.at[j])
        g = j // 2
        kv = slice(HEAD * g, HEAD * (g + 1))
        heads = [slice(0, HEAD), slice(HEAD, 2 * HEAD)]
        for b in range(4):

            @pl.when(hi == b // 2)
            def _(b=b, j=j, kv=kv, heads=heads):
                blocks = COLUMN_BLOCKS[b]
                rows = slice(BLOCK * (b % 2), BLOCK * (b % 2 + 1))
                queries = jnp.concatenate([eq[j][rows, h] for h in heads], axis=0)
                grads = jnp.concatenate([eg[j][rows, h] for h in heads], axis=0)
                keys = jnp.concatenate([ek[BLOCK * n : BLOCK * (n + 1), kv] for n in blocks], axis=0)
                values = jnp.concatenate([ev[BLOCK * n : BLOCK * (n + 1), kv] for n in blocks], axis=0)
                mask = ebias[BIAS_START[b] : BIAS_START[b] + BLOCK * len(blocks), :]
                attn, gq, dkp, dvp = attend(
                    queries, grads, keys, values, jnp.concatenate([mask] * 2, axis=1)
                )
                for n, h in enumerate(heads):
                    ea[j, rows, h] = attn[BLOCK * n : BLOCK * (n + 1)]
                    egq[j, rows, h] = gq[BLOCK * n : BLOCK * (n + 1)]
                for ref, value in ((edk, dkp), (edv, dvp)):
                    for n, cb in enumerate(blocks):
                        ref[BLOCK * cb : BLOCK * (cb + 1), kv] += value[BLOCK * n : BLOCK * (n + 1)]

        if j % 2 == 1:

            @pl.when(hi == 1)
            def _(g=g, kv=kv):
                esk[g] = (edk[0:256, kv] * SCALE).astype(jnp.bfloat16)
                esv[g] = edv[0:256, kv].astype(jnp.bfloat16)
                send(esk.at[g], erk.at[g], s_ep.at[0, g], r_ep.at[0, g], across(0))
                send(esv.at[g], erv.at[g], s_ep.at[1, g], r_ep.at[1, g], across(0))

        exchange(lambda n, j=j: a_even(n, j))

        if j == 1:
            wait(rpk, r_rs.at[0])
            wait(rpv, r_rs.at[1])
            for t in range(2):
                rows = at((SIDE * t + x) * ROWS, ROWS)
                others = [ref[n, :, t].astype(jnp.float32) for ref in (rpk, rpv) for n in range(3)]
                ogk[:, t] = (odk[:, rows, :] * SCALE + others[0] + others[1] + others[2]).astype(
                    jnp.bfloat16
                )
                ogv[:, t] = (odv[:, rows, :] + others[3] + others[4] + others[5]).astype(jnp.bfloat16)
            exchange(None, kv_odd_out)

    @pl.when(hi == 0)
    def _():
        for g in range(2):
            kv = slice(HEAD * g, HEAD * (g + 1))
            wait(erk.at[g], r_ep.at[0, g])
            wait(erv.at[g], r_ep.at[1, g])
            egk[:, kv] = (edk[0:256, kv] * SCALE + erk[g].astype(jnp.float32)).astype(jnp.bfloat16)
            egv[:, kv] = (edv[0:256, kv] + erv[g].astype(jnp.float32)).astype(jnp.bfloat16)

    @pl.when(hi == 1)
    def _():
        egk[...] = (edk[256:512] * SCALE).astype(jnp.bfloat16)
        egv[...] = edv[256:512].astype(jnp.bfloat16)

    exchange(kv_even_out)

    three = 3 * ROWS
    for j in range(E_CHUNKS):
        wait(eq[j].at[0:three, :], s_eq.at[j])
        wait(eg[j].at[0:three, :], s_eg.at[j])
        wait(ea.at[j, 0:three, :], s_ea.at[j])
        wait(egq.at[j, 0:three, :], s_egq.at[j])
    for j in range(O_CHUNKS):
        wait(oq[j].at[:, 0 : three // 2, :], s_oq.at[j])
        wait(og[j].at[:, 0 : three // 2, :], s_og.at[j])
        wait(oa.at[j, :, 0 : three // 2, :], s_oa.at[j])
        wait(ogq.at[j, :, 0 : three // 2, :], s_ogq.at[j])
    for n in range(4):
        wait(ek.at[0:three, :], s_kv.at[n])
        wait(ek.at[0:three, :], s_gkv.at[n])
    for n in range(2):
        wait(ok.at[:, 0 : 2 * three, :], s_all.at[n])
        wait(opk.at[0:3], s_rs.at[n])

    @pl.when(hi == 0)
    def _():
        for n in range(2):
            wait(ek.at[first, :], s_fwd.at[n])

    @pl.when(hi == 1)
    def _():
        for n in range(2):
            for g in range(2):
                wait(esk.at[g], s_ep.at[n, g])

    for n, ref in enumerate((attn_out, gq_out, gk_out, gv_out)):
        wait(ref, r_out.at[n])


def finish_kernel(*refs):
    ins, outs, sem = refs[:4], refs[4:8], refs[8]
    for n in range(4):
        pltpu.make_async_copy(ins[n], outs[n], sem.at[n]).start()
    for n in range(4):
        pltpu.make_async_copy(ins[n], outs[n], sem.at[n]).wait()


def finish(arrays):
    anywhere = pl.BlockSpec(memory_space=pl.ANY)
    return pl.pallas_call(
        finish_kernel,
        out_shape=tuple(jax.ShapeDtypeStruct(a.shape, a.dtype) for a in arrays),
        in_specs=[anywhere] * 4,
        out_specs=(anywhere,) * 4,
        scratch_shapes=[pltpu.SemaphoreType.DMA((4,))],
    )(*[pltpu.with_memory_space_constraint(x, pltpu.VMEM) for x in arrays])


def shards(query_proj, key_proj, value_proj, grad_attn, doc_lengths, mask_tiles, pair_flags):
    bf16, f32 = jnp.bfloat16, jnp.float32
    dma, vmem = pltpu.SemaphoreType.DMA, pltpu.VMEM
    anywhere = pl.BlockSpec(memory_space=pl.ANY)
    scalars = (doc_lengths.T, jnp.transpose(mask_tiles, (1, 2, 0)), pair_flags)
    rows = SIDE * ROWS
    even_kv, odd_kv = vmem((LENGTH, PAIR), bf16), vmem((2, LENGTH, PAIR), bf16)
    even_a = vmem((E_CHUNKS, rows, E_WIDTH), bf16)
    odd_a = vmem((O_CHUNKS, 2, 2 * ROWS, O_WIDTH), bf16)
    even_d, odd_d = vmem((LENGTH, PAIR), f32), vmem((2, LENGTH, PAIR), f32)
    even_part, even_g = vmem((2, rows, HEAD), bf16), vmem((rows, PAIR), bf16)
    odd_part, odd_recv = vmem((4, 2, 2, ROWS, PAIR), bf16), vmem((3, 2, 2, ROWS, PAIR), bf16)
    odd_g = vmem((2, 2, ROWS, PAIR), bf16)
    return finish(pl.pallas_call(
        kernel,
        out_shape=tuple(
            jax.ShapeDtypeStruct(a.shape, bf16)
            for a in (query_proj, query_proj, key_proj, value_proj)
        ),
        in_specs=[anywhere] * 7,
        out_specs=(anywhere,) * 4,
        scratch_shapes=[
            even_kv, even_kv, odd_kv, odd_kv, even_a, even_a, odd_a, odd_a,
            even_d, even_d, odd_d, odd_d,
            vmem((6 * BLOCK, BLOCK), f32), vmem((2, 576, BLOCK), f32),
            even_part, even_part, even_part, even_part, even_g, even_g,
            odd_part, odd_part, odd_recv, odd_recv, odd_g, odd_g,
            *[pltpu.SMEM(a.shape, a.dtype) for a in scalars], dma((3,)),
            dma((E_CHUNKS,)), dma((E_CHUNKS,)), dma((O_CHUNKS,)), dma((O_CHUNKS,)),
            dma((4,)), dma((2,)), dma((2,)), dma((2, 2)), dma((2,)), dma((4,)),
            dma((E_CHUNKS,)), dma((E_CHUNKS,)), dma((O_CHUNKS,)), dma((O_CHUNKS,)),
            dma((4,)), dma((2,)), dma((2,)), dma((2, 2)), dma((2,)),
            dma((E_CHUNKS,)), dma((E_CHUNKS,)), dma((O_CHUNKS,)), dma((O_CHUNKS,)), dma((4,)),
            *[vmem((rows, E_WIDTH), bf16)] * (2 * E_CHUNKS),
            *[vmem((2, 2 * ROWS, O_WIDTH), bf16)] * (2 * O_CHUNKS),
        ],
        compiler_params=pltpu.CompilerParams(
            collective_id=0, has_side_effects=True, vmem_limit_bytes=48 * 2**20
        ),
    )(*[
        pltpu.with_memory_space_constraint(x, pltpu.HBM)
        for x in (query_proj, key_proj, value_proj, grad_attn, *scalars)
    ]))


def solution(mesh):
    split = P("dp", "ctx", None)
    return jax.shard_map(
        shards,
        mesh=mesh,
        in_specs=(split,) * 4 + (P(),) * 3,
        out_specs=(split,) * 4,
        check_vma=False,
    )
```

```python
import functools
import math

import jax
import jax.numpy as jnp
from jax import lax
from jax.experimental import pallas as pl
from jax.experimental.pallas import tpu as pltpu
from jax.sharding import PartitionSpec as P

MESH = pl.DeviceIdType.MESH
HEAD = 128
RATIO = 4
ROWS = 64
LENGTH = 512
BLOCK = 128
SIDE = 4
PAIR = 2 * HEAD
QPAIR = RATIO * PAIR
E_CHUNKS = 4
E_WIDTH = QPAIR // E_CHUNKS
O_CHUNKS = 2
O_WIDTH = QPAIR // O_CHUNKS
SCALE = HEAD ** (-0.5)
EXP2_SCALE = SCALE / math.log(2.0)
COLUMN_BLOCKS = ((0,), (0, 1), (0, 1, 2), (0, 2, 3))
BIAS_START = (0, 128, 0, 384)
NT_DIMS = (((1,), (1,)), ((), ()))
TN_DIMS = (((0,), (0,)), ((), ()))
NN_DIMS = (((1,), (0,)), ((), ()))
STEPS = (1, 3, 2)


def mm(a, b, dims):
    return lax.dot_general(a, b, dims, preferred_element_type=jnp.float32)


def attend(queries, grads, keys, values, mask):
    scores = mm(keys, queries, NT_DIMS) + mask
    peak = jnp.max(scores, axis=0, keepdims=True)
    expd = jnp.exp2((scores - peak) * EXP2_SCALE)
    probs = expd * (1.0 / jnp.sum(expd, axis=0, keepdims=True))
    probs_b = probs.astype(jnp.bfloat16)
    dprobs = mm(values, grads, NT_DIMS)
    delta = jnp.sum(probs * dprobs, axis=0, keepdims=True)
    dscores = (probs * (dprobs - delta)).astype(jnp.bfloat16)
    attn = mm(probs_b, values, TN_DIMS).astype(jnp.bfloat16)
    gq = (mm(dscores, keys, TN_DIMS) * SCALE).astype(jnp.bfloat16)
    return attn, gq, mm(dscores, queries, NN_DIMS), mm(probs_b, grads, NN_DIMS)


def kernel(
    q_in, k_in, v_in, g_in, lengths_in, tiles_in, flags_in,
    attn_out, gq_out, gk_out, gv_out,
    ek, ev, ok, ov, ea, egq, oa, ogq, edk, edv, odk, odv, ebias, obias,
    esk, esv, erk, erv, egk, egv, opk, opv, rpk, rpv, ogk, ogv, rtk, rtv, ctk, ctv, r_rt, s_ct,
    lengths, tiles, flags, scalar_sem,
    r_eq, r_eg, r_oq, r_og, r_kv, r_all, r_fwd, r_ep, r_rs, r_out, r_rel, s_rel,
    s_eq, s_eg, s_oq, s_og, s_kv, s_all, s_fwd, s_ep, s_rs,
    s_ea, s_egq, s_oa, s_ogq, s_gkv,
    *bufs,
):
    eq, eg = bufs[0:E_CHUNKS], bufs[E_CHUNKS : 2 * E_CHUNKS]
    oq, og = bufs[2 * E_CHUNKS : 2 * E_CHUNKS + O_CHUNKS], bufs[2 * E_CHUNKS + O_CHUNKS :]
    dp = lax.axis_index("dp")
    c = lax.axis_index("ctx")
    half = lax.axis_size("dp") // 2
    low = dp // half
    zc = dp % half
    hi = c // SIDE
    x = c % SIDE
    y = 2 * hi + low

    def along_x(step):
        xn = (x + step) % SIDE
        return xn, {"dp": dp, "ctx": hi * SIDE + xn}

    def along_y(step):
        yn = (y + step) % SIDE
        return yn, {"dp": (yn % 2) * half + zc, "ctx": (yn // 2) * SIDE + x}

    def across(device_hi):
        return {"dp": dp, "ctx": device_hi * SIDE + x}

    scalar_copies = [
        pltpu.make_async_copy(src, dst, scalar_sem.at[n])
        for n, (src, dst) in enumerate(((lengths_in, lengths), (tiles_in, tiles), (flags_in, flags)))
    ]
    for copy in scalar_copies:
        copy.start()

    barrier = pltpu.get_barrier_semaphore()
    for step in STEPS:
        for along in (along_x, along_y):
            pl.semaphore_signal(barrier, inc=1, device_id=along(step)[1], device_id_type=MESH)
    pl.semaphore_wait(barrier, 6)

    def send(src, dst, send_sem, recv_sem, device):
        pltpu.make_async_remote_copy(
            src_ref=src, dst_ref=dst, send_sem=send_sem, recv_sem=recv_sem,
            device_id=device, device_id_type=MESH,
        ).start()

    def keep(src, dst, _, recv_sem):
        pltpu.make_async_copy(src, dst, recv_sem).start()

    def wait(ref, sem):
        pltpu.make_async_copy(ref, ref, sem).wait()

    def at(start, size):
        return pl.ds(pl.multiple_of(start, size), size)

    rows_c = at(c * ROWS, ROWS)
    rows_x = at(x * ROWS, ROWS)
    rows_hi = at(hi * ROWS, ROWS)

    def kv_even(n):
        cols = at(n * PAIR, PAIR)
        return [
            (k_in.at[0, :, cols], ek.at[rows_c, :], s_kv.at[0], r_kv.at[0]),
            (v_in.at[0, :, cols], ev.at[rows_c, :], s_kv.at[1], r_kv.at[1]),
        ]

    def kv_odd(n):
        cols = at(n * PAIR, PAIR)
        return [
            (k_in.at[1, :, cols], ok.at[low, rows_c, :], s_kv.at[2], r_kv.at[2]),
            (v_in.at[1, :, cols], ov.at[low, rows_c, :], s_kv.at[3], r_kv.at[3]),
        ]

    def q_even(n, j):
        cols = at(n * QPAIR + j * E_WIDTH, E_WIDTH)
        return [
            (q_in.at[0, :, cols], eq[j].at[rows_x, :], s_eq.at[j], r_eq.at[j]),
            (g_in.at[0, :, cols], eg[j].at[rows_x, :], s_eg.at[j], r_eg.at[j]),
        ]

    def q_odd(n, j):
        cols = at(n * QPAIR + j * O_WIDTH, O_WIDTH)
        return [
            (q_in.at[1, :, cols], oq[j].at[low, rows_hi, :], s_oq.at[j], r_oq.at[j]),
            (g_in.at[1, :, cols], og[j].at[low, rows_hi, :], s_og.at[j], r_og.at[j]),
        ]

    def exchange(even=None, odd=None):
        for step in STEPS:
            if odd is not None:
                n, device = along_y(step)
                for item in odd(n):
                    send(*item, device)
            if even is not None:
                n, device = along_x(step)
                for item in even(n):
                    send(*item, device)
        for item in (odd(y) if odd is not None else []) + (even(x) if even is not None else []):
            keep(*item)

    exchange(kv_even, kv_odd)
    exchange(lambda n: q_even(n, 0), lambda n: q_odd(n, 0))

    for copy in scalar_copies:
        copy.wait()
    flag = jnp.where(flags[dp] == 1, 1, 0)
    lane = lax.broadcasted_iota(jnp.int32, (BLOCK, BLOCK), 1)
    sub = lax.broadcasted_iota(jnp.int32, (BLOCK, BLOCK), 0)

    def segment_ends(seq):
        ends = []
        total = lengths[0, seq]
        for d in range(1, 8):
            ends.append(total)
            total = total + lengths[d, seq]
        return ends

    def addend(ends, row, col, tile):
        row_doc = sum((row >= e).astype(jnp.int32) for e in ends)
        col_doc = sum((col >= e).astype(jnp.int32) for e in ends)
        allowed = (col <= row) & ((col_doc == row_doc) | (col_doc == 0)) & (tile == 1)
        return jnp.where(allowed, 0.0, -1e30)

    wait(ok.at[:, 0 : 2 * ROWS, :], r_kv.at[2])
    wait(ov.at[:, 0 : 2 * ROWS, :], r_kv.at[3])
    for side, step in enumerate((1, 3)):
        _, device = along_x(step)
        for t in range(2):
            part = at((SIDE * t + x) * ROWS, ROWS)
            for n, ref in enumerate((ok, ov)):
                here = ref.at[:, part, :]
                send(here, here, s_all.at[n], r_all.at[2 * side + n], device)
    wait(ek.at[0 : SIDE * ROWS, :], r_kv.at[0])
    wait(ev.at[0 : SIDE * ROWS, :], r_kv.at[1])

    first = pl.ds(0, SIDE * ROWS)

    @pl.when(hi == 0)
    def _():
        for n, ref in enumerate((ek, ev)):
            send(ref.at[first, :], ref.at[first, :], s_fwd.at[n], r_fwd.at[n], across(1))

    exchange(lambda n: q_even(n, 1), lambda n: q_odd(n, 1))

    for b in range(4):

        @pl.when(hi == b // 2)
        def _(b=b):
            seq = 2 * dp
            ends = segment_ends(seq)
            row = lane + BLOCK * b
            for n, cb in enumerate(COLUMN_BLOCKS[b]):
                top, bottom = (
                    jnp.where(
                        lane < 64,
                        tiles[2 * b, 2 * cb + m, seq],
                        tiles[2 * b + 1, 2 * cb + m, seq],
                    )
                    for m in range(2)
                )
                start = BIAS_START[b] + BLOCK * n
                ebias[start : start + BLOCK, :] = addend(
                    ends, row, sub + BLOCK * cb, jnp.where(sub < 64, top, bottom)
                )

    for side, step in enumerate((1, 3)):
        _, device = along_x(step)
        for n, ref in enumerate((ok, ov)):
            wait(ref.at[:, 0 : 2 * ROWS, :], r_all.at[2 * side + n])
            for t in range(2):
                part = at((SIDE * t + (x + 4 - step) % SIDE) * ROWS, ROWS)
                here = ref.at[side, part, :]
                send(here, here, s_rel.at[n], r_rel.at[2 * side + n], device)

    for j in range(2, E_CHUNKS):
        exchange(lambda n, j=j: q_even(n, j))

    def source(slot):
        return slot + flag - 2 * slot * flag

    near = x + 2

    @pl.loop(0, 2)
    def _(slot):
        seq = 2 * (source(slot) * half + zc) + 1
        ends = segment_ends(seq)
        inner = lane % ROWS
        for t, start in ((0, 0), (0, BLOCK), (1, 2 * BLOCK)):
            row_tile = SIDE * t + x
            cb = start // BLOCK % 2
            tile = jnp.where(sub < 64, tiles[row_tile, 2 * cb, seq], tiles[row_tile, 2 * cb + 1, seq])
            obias[slot, start : start + BLOCK, :] = addend(
                ends, inner + row_tile * ROWS, sub + BLOCK * cb, tile
            )
        for m in range(3):
            start = 3 * BLOCK + ROWS * m
            tile = jnp.zeros_like(sub[:ROWS]) + tiles[SIDE + x, near + m, seq]
            obias[slot, start : start + ROWS, :] = addend(
                ends, inner[:ROWS] + (SIDE + x) * ROWS, sub[:ROWS] + (near + m) * ROWS, tile
            )

    for ref in (edk, edv, odk, odv):
        ref[...] = jnp.zeros_like(ref)

    def a_even(n, j):
        rows, cols = at(n * ROWS, ROWS), at(x * QPAIR + j * E_WIDTH, E_WIDTH)
        return [
            (ea.at[j, rows, :], attn_out.at[0, :, cols], s_ea.at[j], r_out.at[0]),
            (egq.at[j, rows, :], gq_out.at[0, :, cols], s_egq.at[j], r_out.at[1]),
        ]

    def a_odd(n, j):
        rows, cols = at((n // 2) * ROWS, ROWS), at(y * QPAIR + j * O_WIDTH, O_WIDTH)
        return [
            (oa.at[j, n % 2, rows, :], attn_out.at[1, :, cols], s_oa.at[j], r_out.at[0]),
            (ogq.at[j, n % 2, rows, :], gq_out.at[1, :, cols], s_ogq.at[j], r_out.at[1]),
        ]

    def kv_even_out(n):
        rows, cols = at(n * ROWS, ROWS), at(x * PAIR, PAIR)
        return [
            (egk.at[rows, :], gk_out.at[0, :, cols], s_gkv.at[0], r_out.at[2]),
            (egv.at[rows, :], gv_out.at[0, :, cols], s_gkv.at[1], r_out.at[3]),
        ]

    def kv_odd_out(n):
        cols = at(y * PAIR, PAIR)
        return [
            (ogk.at[n % 2, n // 2], gk_out.at[1, :, cols], s_gkv.at[2], r_out.at[2]),
            (ogv.at[n % 2, n // 2], gv_out.at[1, :, cols], s_gkv.at[3], r_out.at[3]),
        ]

    late = pl.ds(pl.multiple_of(near * ROWS, ROWS), 3 * ROWS)
    for side in range(2):
        for n, ref in enumerate((ok, ov)):
            wait(ref.at[side, 0 : 2 * ROWS, :], r_rel.at[2 * side + n])

    for j in range(O_CHUNKS):
        wait(oq[j], r_oq.at[j])
        wait(og[j], r_og.at[j])
        kv = slice(HEAD * j, HEAD * (j + 1))
        heads = [slice(HEAD * h, HEAD * (h + 1)) for h in range(RATIO)]

        @pl.loop(0, 2)
        def _(slot, j=j, kv=kv, heads=heads):
            u = source(slot)
            for t in range(2):
                rows = slice(ROWS * t, ROWS * (t + 1))
                queries = jnp.concatenate([oq[j][u, rows, h] for h in heads], axis=0)
                grads = jnp.concatenate([og[j][u, rows, h] for h in heads], axis=0)
                if t == 0:
                    keys, values = ok[u, 0:256, kv], ov[u, 0:256, kv]
                    mask = obias[slot, 0:256, :]
                else:
                    keys = jnp.concatenate([ok[u, 0:128, kv], ok[u, late, kv]], axis=0)
                    values = jnp.concatenate([ov[u, 0:128, kv], ov[u, late, kv]], axis=0)
                    mask = obias[slot, 256:576, :]
                attn, gq, dkp, dvp = attend(
                    queries, grads, keys, values, jnp.concatenate([mask] * 2, axis=1)
                )
                for n, h in enumerate(heads):
                    oa[j, slot, rows, h] = attn[ROWS * n : ROWS * (n + 1)]
                    ogq[j, slot, rows, h] = gq[ROWS * n : ROWS * (n + 1)]
                for ref, value in ((odk, dkp), (odv, dvp)):
                    if t == 0:
                        ref[slot, 0:256, kv] += value
                    else:
                        ref[slot, 0:128, kv] += value[:128]
                        ref[slot, late, kv] += value[128:]

        exchange(None, lambda n, j=j: a_odd(n, j))

    for t in range(8):
        rows = slice(ROWS * t, ROWS * (t + 1))
        opk[t % SIDE, :, t // SIDE] = (odk[:, rows] * SCALE).astype(jnp.bfloat16)
        opv[t % SIDE, :, t // SIDE] = odv[:, rows].astype(jnp.bfloat16)
    far = (x + 2) % SIDE
    for n, (op, rt, rp) in enumerate(((opk, rtk, rpk), (opv, rtv, rpv))):
        for side, step in enumerate((1, 3)):
            near_x, device = along_x(step)
            send(op.at[far, side], rt.at[side], s_rs.at[n], r_rt.at[n], device)
            send(op.at[near_x, 1 - side], rp.at[side, 1 - side], s_rs.at[n], r_rs.at[n], device)

    @pl.when(hi == 1)
    def _():
        wait(ek.at[first, :], r_fwd.at[0])
        wait(ev.at[first, :], r_fwd.at[1])

    for j in range(E_CHUNKS):
        wait(eq[j], r_eq.at[j])
        wait(eg[j], r_eg.at[j])
        g = j // 2
        kv = slice(HEAD * g, HEAD * (g + 1))
        heads = [slice(0, HEAD), slice(HEAD, 2 * HEAD)]
        for b in range(4):

            @pl.when(hi == b // 2)
            def _(b=b, j=j, kv=kv, heads=heads):
                blocks = COLUMN_BLOCKS[b]
                rows = slice(BLOCK * (b % 2), BLOCK * (b % 2 + 1))
                queries = jnp.concatenate([eq[j][rows, h] for h in heads], axis=0)
                grads = jnp.concatenate([eg[j][rows, h] for h in heads], axis=0)
                keys = jnp.concatenate([ek[BLOCK * n : BLOCK * (n + 1), kv] for n in blocks], axis=0)
                values = jnp.concatenate([ev[BLOCK * n : BLOCK * (n + 1), kv] for n in blocks], axis=0)
                mask = ebias[BIAS_START[b] : BIAS_START[b] + BLOCK * len(blocks), :]
                attn, gq, dkp, dvp = attend(
                    queries, grads, keys, values, jnp.concatenate([mask] * 2, axis=1)
                )
                for n, h in enumerate(heads):
                    ea[j, rows, h] = attn[BLOCK * n : BLOCK * (n + 1)]
                    egq[j, rows, h] = gq[BLOCK * n : BLOCK * (n + 1)]
                for ref, value in ((edk, dkp), (edv, dvp)):
                    for n, cb in enumerate(blocks):
                        ref[BLOCK * cb : BLOCK * (cb + 1), kv] += value[BLOCK * n : BLOCK * (n + 1)]

        if j % 2 == 1:

            @pl.when(hi == 1)
            def _(g=g, kv=kv):
                esk[g] = (edk[0:256, kv] * SCALE).astype(jnp.bfloat16)
                esv[g] = edv[0:256, kv].astype(jnp.bfloat16)
                send(esk.at[g], erk.at[g], s_ep.at[0, g], r_ep.at[0, g], across(0))
                send(esv.at[g], erv.at[g], s_ep.at[1, g], r_ep.at[1, g], across(0))

        exchange(lambda n, j=j: a_even(n, j))

        if j == 0:
            for n, (ref, rt, ct, rp, scale) in enumerate(
                ((odk, rtk, ctk, rpk, SCALE), (odv, rtv, ctv, rpv, 1.0))
            ):
                wait(rt, r_rt.at[n])
                for side, step in enumerate((1, 3)):
                    near_x, device = along_x(step)
                    for t in range(2):
                        rows = at((SIDE * t + near_x) * ROWS, ROWS)
                        ct[side, t] = (
                            ref[side, rows, :] * scale + rt[side, t].astype(jnp.float32)
                        ).astype(jnp.bfloat16)
                    send(ct.at[side], rp.at[side, side], s_ct.at[n], r_rs.at[n], device)

        if j == 2:
            wait(rpk, r_rs.at[0])
            wait(rpv, r_rs.at[1])
            for t in range(2):
                rows = at((SIDE * t + x) * ROWS, ROWS)
                others = [ref[n, :, t].astype(jnp.float32) for ref in (rpk, rpv) for n in range(2)]
                ogk[:, t] = (odk[:, rows, :] * SCALE + others[0] + others[1]).astype(
                    jnp.bfloat16
                )
                ogv[:, t] = (odv[:, rows, :] + others[2] + others[3]).astype(jnp.bfloat16)
            exchange(None, kv_odd_out)

    @pl.when(hi == 0)
    def _():
        for g in range(2):
            kv = slice(HEAD * g, HEAD * (g + 1))
            wait(erk.at[g], r_ep.at[0, g])
            wait(erv.at[g], r_ep.at[1, g])
            egk[:, kv] = (edk[0:256, kv] * SCALE + erk[g].astype(jnp.float32)).astype(jnp.bfloat16)
            egv[:, kv] = (edv[0:256, kv] + erv[g].astype(jnp.float32)).astype(jnp.bfloat16)

    @pl.when(hi == 1)
    def _():
        egk[...] = (edk[256:512] * SCALE).astype(jnp.bfloat16)
        egv[...] = edv[256:512].astype(jnp.bfloat16)

    exchange(kv_even_out)

    three = 3 * ROWS
    for j in range(E_CHUNKS):
        wait(eq[j].at[0:three, :], s_eq.at[j])
        wait(eg[j].at[0:three, :], s_eg.at[j])
        wait(ea.at[j, 0:three, :], s_ea.at[j])
        wait(egq.at[j, 0:three, :], s_egq.at[j])
    for j in range(O_CHUNKS):
        wait(oq[j].at[:, 0 : three // 2, :], s_oq.at[j])
        wait(og[j].at[:, 0 : three // 2, :], s_og.at[j])
        wait(oa.at[j, :, 0 : three // 2, :], s_oa.at[j])
        wait(ogq.at[j, :, 0 : three // 2, :], s_ogq.at[j])
    for n in range(4):
        wait(ek.at[0:three, :], s_kv.at[n])
        wait(ek.at[0:three, :], s_gkv.at[n])
    for n in range(2):
        wait(ok.at[:, 0 : 4 * ROWS, :], s_all.at[n])
        wait(ok.at[:, 0 : 2 * ROWS, :], s_rel.at[n])
        wait(opk.at[0:2], s_rs.at[n])
        wait(ctk, s_ct.at[n])

    @pl.when(hi == 0)
    def _():
        for n in range(2):
            wait(ek.at[first, :], s_fwd.at[n])

    @pl.when(hi == 1)
    def _():
        for n in range(2):
            for g in range(2):
                wait(esk.at[g], s_ep.at[n, g])

    for n, ref in enumerate((attn_out, gq_out, gk_out, gv_out)):
        wait(ref, r_out.at[n])


def finish_kernel(*refs):
    ins, outs, sem = refs[:4], refs[4:8], refs[8]
    for n in range(4):
        pltpu.make_async_copy(ins[n], outs[n], sem.at[n]).start()
    for n in range(4):
        pltpu.make_async_copy(ins[n], outs[n], sem.at[n]).wait()


def finish(arrays):
    anywhere = pl.BlockSpec(memory_space=pl.ANY)
    return pl.pallas_call(
        finish_kernel,
        out_shape=tuple(jax.ShapeDtypeStruct(a.shape, a.dtype) for a in arrays),
        in_specs=[anywhere] * 4,
        out_specs=(anywhere,) * 4,
        scratch_shapes=[pltpu.SemaphoreType.DMA((4,))],
    )(*[pltpu.with_memory_space_constraint(x, pltpu.VMEM) for x in arrays])


def shards(query_proj, key_proj, value_proj, grad_attn, doc_lengths, mask_tiles, pair_flags):
    bf16, f32 = jnp.bfloat16, jnp.float32
    dma, vmem = pltpu.SemaphoreType.DMA, pltpu.VMEM
    anywhere = pl.BlockSpec(memory_space=pl.ANY)
    scalars = (doc_lengths.T, jnp.transpose(mask_tiles, (1, 2, 0)), pair_flags)
    rows = SIDE * ROWS
    even_kv, odd_kv = vmem((LENGTH, PAIR), bf16), vmem((2, LENGTH, PAIR), bf16)
    even_a = vmem((E_CHUNKS, rows, E_WIDTH), bf16)
    odd_a = vmem((O_CHUNKS, 2, 2 * ROWS, O_WIDTH), bf16)
    even_d, odd_d = vmem((LENGTH, PAIR), f32), vmem((2, LENGTH, PAIR), f32)
    even_part, even_g = vmem((2, rows, HEAD), bf16), vmem((rows, PAIR), bf16)
    odd_part, odd_recv = vmem((4, 2, 2, ROWS, PAIR), bf16), vmem((2, 2, 2, ROWS, PAIR), bf16)
    odd_g = vmem((2, 2, ROWS, PAIR), bf16)
    return finish(pl.pallas_call(
        kernel,
        out_shape=tuple(
            jax.ShapeDtypeStruct(a.shape, bf16)
            for a in (query_proj, query_proj, key_proj, value_proj)
        ),
        in_specs=[anywhere] * 7,
        out_specs=(anywhere,) * 4,
        scratch_shapes=[
            even_kv, even_kv, odd_kv, odd_kv, even_a, even_a, odd_a, odd_a,
            even_d, even_d, odd_d, odd_d,
            vmem((6 * BLOCK, BLOCK), f32), vmem((2, 576, BLOCK), f32),
            even_part, even_part, even_part, even_part, even_g, even_g,
            odd_part, odd_part, odd_recv, odd_recv, odd_g, odd_g,
            odd_g, odd_g, odd_g, odd_g, dma((2,)), dma((2,)),
            *[pltpu.SMEM(a.shape, a.dtype) for a in scalars], dma((3,)),
            dma((E_CHUNKS,)), dma((E_CHUNKS,)), dma((O_CHUNKS,)), dma((O_CHUNKS,)),
            dma((4,)), dma((4,)), dma((2,)), dma((2, 2)), dma((2,)), dma((4,)), dma((4,)), dma((2,)),
            dma((E_CHUNKS,)), dma((E_CHUNKS,)), dma((O_CHUNKS,)), dma((O_CHUNKS,)),
            dma((4,)), dma((2,)), dma((2,)), dma((2, 2)), dma((2,)),
            dma((E_CHUNKS,)), dma((E_CHUNKS,)), dma((O_CHUNKS,)), dma((O_CHUNKS,)), dma((4,)),
            *[vmem((rows, E_WIDTH), bf16)] * (2 * E_CHUNKS),
            *[vmem((2, 2 * ROWS, O_WIDTH), bf16)] * (2 * O_CHUNKS),
        ],
        compiler_params=pltpu.CompilerParams(
            collective_id=0, has_side_effects=True, vmem_limit_bytes=48 * 2**20
        ),
    )(*[
        pltpu.with_memory_space_constraint(x, pltpu.HBM)
        for x in (query_proj, key_proj, value_proj, grad_attn, *scalars)
    ]))


def solution(mesh):
    split = P("dp", "ctx", None)
    return jax.shard_map(
        shards,
        mesh=mesh,
        in_specs=(split,) * 4 + (P(),) * 3,
        out_specs=(split,) * 4,
        check_vma=False,
    )
```

```python
import functools
import math

import jax
import jax.numpy as jnp
from jax import lax
from jax.experimental import pallas as pl
from jax.experimental.pallas import tpu as pltpu
from jax.sharding import PartitionSpec as P

MESH = pl.DeviceIdType.MESH
HEAD = 128
RATIO = 4
ROWS = 64
LENGTH = 512
BLOCK = 128
SIDE = 4
PAIR = 2 * HEAD
QPAIR = RATIO * PAIR
E_CHUNKS = 4
E_WIDTH = QPAIR // E_CHUNKS
O_CHUNKS = 2
O_WIDTH = QPAIR // O_CHUNKS
SCALE = HEAD ** (-0.5)
EXP2_SCALE = SCALE / math.log(2.0)
COLUMN_BLOCKS = ((0,), (0, 1), (0, 1, 2), (0, 2, 3))
BIAS_START = (0, 128, 0, 384)
NT_DIMS = (((1,), (1,)), ((), ()))
TN_DIMS = (((0,), (0,)), ((), ()))
NN_DIMS = (((1,), (0,)), ((), ()))
STEPS = (1, 3, 2)


def mm(a, b, dims):
    return lax.dot_general(a, b, dims, preferred_element_type=jnp.float32)


def attend(queries, grads, keys, values, mask):
    scores = mm(keys, queries, NT_DIMS) + mask
    peak = jnp.max(scores, axis=0, keepdims=True)
    expd = jnp.exp2((scores - peak) * EXP2_SCALE)
    probs = expd * (1.0 / jnp.sum(expd, axis=0, keepdims=True))
    probs_b = probs.astype(jnp.bfloat16)
    dprobs = mm(values, grads, NT_DIMS)
    delta = jnp.sum(probs * dprobs, axis=0, keepdims=True)
    dscores = (probs * (dprobs - delta)).astype(jnp.bfloat16)
    attn = mm(probs_b, values, TN_DIMS).astype(jnp.bfloat16)
    gq = (mm(dscores, keys, TN_DIMS) * SCALE).astype(jnp.bfloat16)
    return attn, gq, mm(dscores, queries, NN_DIMS), mm(probs_b, grads, NN_DIMS)


def kernel(
    q_in, k_in, v_in, g_in, lengths_in, tiles_in, flags_in,
    attn_out, gq_out, gk_out, gv_out,
    ek, ev, ok, ov, ea, egq, oa, ogq, edk, edv, odk, odv, ebias, obias,
    esk, esv, erk, erv, egk, egv, opk, opv, rpk, rpv, ogk, ogv, rtk, rtv, ctk, ctv, r_rt, s_ct,
    lengths, tiles, flags, scalar_sem,
    r_eq, r_eg, r_oq, r_og, r_kv, r_all, r_fwd, r_ep, r_rs, r_out, r_rel, s_rel,
    s_eq, s_eg, s_oq, s_og, s_kv, s_all, s_fwd, s_ep, s_rs,
    s_ea, s_egq, s_oa, s_ogq, s_gkv,
    *bufs,
):
    eq, eg = bufs[0:E_CHUNKS], bufs[E_CHUNKS : 2 * E_CHUNKS]
    oq, og = bufs[2 * E_CHUNKS : 2 * E_CHUNKS + O_CHUNKS], bufs[2 * E_CHUNKS + O_CHUNKS :]
    dp = lax.axis_index("dp")
    c = lax.axis_index("ctx")
    half = lax.axis_size("dp") // 2
    low = dp // half
    zc = dp % half
    hi = c // SIDE
    x = c % SIDE
    y = 2 * hi + low

    def along_x(step):
        xn = (x + step) % SIDE
        return xn, {"dp": dp, "ctx": hi * SIDE + xn}

    def along_y(step):
        yn = (y + step) % SIDE
        return yn, {"dp": (yn % 2) * half + zc, "ctx": (yn // 2) * SIDE + x}

    def across(device_hi):
        return {"dp": dp, "ctx": device_hi * SIDE + x}

    scalar_copies = [
        pltpu.make_async_copy(src, dst, scalar_sem.at[n])
        for n, (src, dst) in enumerate(((lengths_in, lengths), (tiles_in, tiles), (flags_in, flags)))
    ]
    for copy in scalar_copies:
        copy.start()

    barrier = pltpu.get_barrier_semaphore()
    for step in STEPS:
        for along in (along_x, along_y):
            pl.semaphore_signal(barrier, inc=1, device_id=along(step)[1], device_id_type=MESH)
    pl.semaphore_wait(barrier, 6)

    def send(src, dst, send_sem, recv_sem, device):
        pltpu.make_async_remote_copy(
            src_ref=src, dst_ref=dst, send_sem=send_sem, recv_sem=recv_sem,
            device_id=device, device_id_type=MESH,
        ).start()

    def keep(src, dst, _, recv_sem):
        pltpu.make_async_copy(src, dst, recv_sem).start()

    def wait(ref, sem):
        pltpu.make_async_copy(ref, ref, sem).wait()

    def at(start, size):
        return pl.ds(pl.multiple_of(start, size), size)

    rows_c = at(c * ROWS, ROWS)
    rows_x = at(x * ROWS, ROWS)
    rows_hi = at(hi * ROWS, ROWS)

    def kv_even(n):
        cols = at(n * PAIR, PAIR)
        return [
            (k_in.at[0, :, cols], ek.at[rows_c, :], s_kv.at[0], r_kv.at[0]),
            (v_in.at[0, :, cols], ev.at[rows_c, :], s_kv.at[1], r_kv.at[1]),
        ]

    def kv_odd(n):
        cols = at(n * PAIR, PAIR)
        return [
            (k_in.at[1, :, cols], ok.at[low, rows_c, :], s_kv.at[2], r_kv.at[2]),
            (v_in.at[1, :, cols], ov.at[low, rows_c, :], s_kv.at[3], r_kv.at[3]),
        ]

    def q_even(n, j):
        cols = at(n * QPAIR + j * E_WIDTH, E_WIDTH)
        return [
            (q_in.at[0, :, cols], eq[j].at[rows_x, :], s_eq.at[j], r_eq.at[j]),
            (g_in.at[0, :, cols], eg[j].at[rows_x, :], s_eg.at[j], r_eg.at[j]),
        ]

    def q_odd(n, j):
        cols = at(n * QPAIR + j * O_WIDTH, O_WIDTH)
        return [
            (q_in.at[1, :, cols], oq[j].at[low, rows_hi, :], s_oq.at[j], r_oq.at[j]),
            (g_in.at[1, :, cols], og[j].at[low, rows_hi, :], s_og.at[j], r_og.at[j]),
        ]

    def exchange(even=None, odd=None):
        for step in STEPS:
            if odd is not None:
                n, device = along_y(step)
                for item in odd(n):
                    send(*item, device)
            if even is not None:
                n, device = along_x(step)
                for item in even(n):
                    send(*item, device)
        for item in (odd(y) if odd is not None else []) + (even(x) if even is not None else []):
            keep(*item)

    exchange(kv_even, kv_odd)
    exchange(lambda n: q_even(n, 0), lambda n: q_odd(n, 0))

    for copy in scalar_copies:
        copy.wait()
    flag = jnp.where(flags[dp] == 1, 1, 0)
    lane = lax.broadcasted_iota(jnp.int32, (BLOCK, BLOCK), 1)
    sub = lax.broadcasted_iota(jnp.int32, (BLOCK, BLOCK), 0)

    def segment_ends(seq):
        ends = []
        total = lengths[0, seq]
        for d in range(1, 8):
            ends.append(total)
            total = total + lengths[d, seq]
        return ends

    def addend(ends, row, col, tile):
        row_doc = sum((row >= e).astype(jnp.int32) for e in ends)
        col_doc = sum((col >= e).astype(jnp.int32) for e in ends)
        allowed = (col <= row) & ((col_doc == row_doc) | (col_doc == 0)) & (tile == 1)
        return jnp.where(allowed, 0.0, -1e30)

    wait(ok.at[:, 0 : 2 * ROWS, :], r_kv.at[2])
    wait(ov.at[:, 0 : 2 * ROWS, :], r_kv.at[3])
    for side, step in enumerate((1, 3)):
        _, device = along_x(step)
        for t in range(2):
            part = at((SIDE * t + x) * ROWS, ROWS)
            for n, ref in enumerate((ok, ov)):
                here = ref.at[:, part, :]
                send(here, here, s_all.at[n], r_all.at[2 * side + n], device)
    wait(ek.at[0 : SIDE * ROWS, :], r_kv.at[0])
    wait(ev.at[0 : SIDE * ROWS, :], r_kv.at[1])

    first = pl.ds(0, SIDE * ROWS)

    @pl.when(hi == 0)
    def _():
        for n, ref in enumerate((ek, ev)):
            send(ref.at[first, :], ref.at[first, :], s_fwd.at[n], r_fwd.at[n], across(1))

    exchange(lambda n: q_even(n, 1), lambda n: q_odd(n, 1))

    for b in range(4):

        @pl.when(hi == b // 2)
        def _(b=b):
            seq = 2 * dp
            ends = segment_ends(seq)
            row = lane + BLOCK * b
            for n, cb in enumerate(COLUMN_BLOCKS[b]):
                top, bottom = (
                    jnp.where(
                        lane < 64,
                        tiles[2 * b, 2 * cb + m, seq],
                        tiles[2 * b + 1, 2 * cb + m, seq],
                    )
                    for m in range(2)
                )
                start = BIAS_START[b] + BLOCK * n
                ebias[start : start + BLOCK, :] = addend(
                    ends, row, sub + BLOCK * cb, jnp.where(sub < 64, top, bottom)
                )

    for side, step in enumerate((1, 3)):
        _, device = along_x(step)
        for n, ref in enumerate((ok, ov)):
            wait(ref.at[:, 0 : 2 * ROWS, :], r_all.at[2 * side + n])
            for t in range(2):
                part = at((SIDE * t + (x + 4 - step) % SIDE) * ROWS, ROWS)
                here = ref.at[side, part, :]
                send(here, here, s_rel.at[n], r_rel.at[2 * side + n], device)

    for j in range(2, E_CHUNKS):
        exchange(lambda n, j=j: q_even(n, j))

    def source(slot):
        return slot + flag - 2 * slot * flag

    near = x + 2

    @pl.loop(0, 2)
    def _(slot):
        seq = 2 * (source(slot) * half + zc) + 1
        ends = segment_ends(seq)
        inner = lane % ROWS
        for t, start in ((0, 0), (0, BLOCK), (1, 2 * BLOCK)):
            row_tile = SIDE * t + x
            cb = start // BLOCK % 2
            tile = jnp.where(sub < 64, tiles[row_tile, 2 * cb, seq], tiles[row_tile, 2 * cb + 1, seq])
            obias[slot, start : start + BLOCK, :] = addend(
                ends, inner + row_tile * ROWS, sub + BLOCK * cb, tile
            )
        for m in range(3):
            start = 3 * BLOCK + ROWS * m
            tile = jnp.zeros_like(sub[:ROWS]) + tiles[SIDE + x, near + m, seq]
            obias[slot, start : start + ROWS, :] = addend(
                ends, inner[:ROWS] + (SIDE + x) * ROWS, sub[:ROWS] + (near + m) * ROWS, tile
            )

    for ref in (edk, edv, odk, odv):
        ref[...] = jnp.zeros_like(ref)

    def a_even(n, j):
        rows, cols = at(n * ROWS, ROWS), at(x * QPAIR + j * E_WIDTH, E_WIDTH)
        return [
            (ea.at[j, rows, :], attn_out.at[0, :, cols], s_ea.at[j], r_out.at[0]),
            (egq.at[j, rows, :], gq_out.at[0, :, cols], s_egq.at[j], r_out.at[1]),
        ]

    def a_odd(n, j):
        rows, cols = at((n // 2) * ROWS, ROWS), at(y * QPAIR + j * O_WIDTH, O_WIDTH)
        return [
            (oa.at[j, n % 2, rows, :], attn_out.at[1, :, cols], s_oa.at[j], r_out.at[0]),
            (ogq.at[j, n % 2, rows, :], gq_out.at[1, :, cols], s_ogq.at[j], r_out.at[1]),
        ]

    def kv_even_out(n):
        rows, cols = at(n * ROWS, ROWS), at(x * PAIR, PAIR)
        return [
            (egk.at[rows, :], gk_out.at[0, :, cols], s_gkv.at[0], r_out.at[2]),
            (egv.at[rows, :], gv_out.at[0, :, cols], s_gkv.at[1], r_out.at[3]),
        ]

    def kv_odd_out(n):
        cols = at(y * PAIR, PAIR)
        return [
            (ogk.at[n % 2, n // 2], gk_out.at[1, :, cols], s_gkv.at[2], r_out.at[2]),
            (ogv.at[n % 2, n // 2], gv_out.at[1, :, cols], s_gkv.at[3], r_out.at[3]),
        ]

    late = pl.ds(pl.multiple_of(near * ROWS, ROWS), 3 * ROWS)
    def odd_ready():
        for side in range(2):
            for n, ref in enumerate((ok, ov)):
                wait(ref.at[side, 0 : 2 * ROWS, :], r_rel.at[2 * side + n])

    def odd_chunk(j):
        wait(oq[j], r_oq.at[j])
        wait(og[j], r_og.at[j])
        kv = slice(HEAD * j, HEAD * (j + 1))
        heads = [slice(HEAD * h, HEAD * (h + 1)) for h in range(RATIO)]

        @pl.loop(0, 2)
        def _(slot, j=j, kv=kv, heads=heads):
            u = source(slot)
            for t in range(2):
                rows = slice(ROWS * t, ROWS * (t + 1))
                queries = jnp.concatenate([oq[j][u, rows, h] for h in heads], axis=0)
                grads = jnp.concatenate([og[j][u, rows, h] for h in heads], axis=0)
                if t == 0:
                    keys, values = ok[u, 0:256, kv], ov[u, 0:256, kv]
                    mask = obias[slot, 0:256, :]
                else:
                    keys = jnp.concatenate([ok[u, 0:128, kv], ok[u, late, kv]], axis=0)
                    values = jnp.concatenate([ov[u, 0:128, kv], ov[u, late, kv]], axis=0)
                    mask = obias[slot, 256:576, :]
                attn, gq, dkp, dvp = attend(
                    queries, grads, keys, values, jnp.concatenate([mask] * 2, axis=1)
                )
                for n, h in enumerate(heads):
                    oa[j, slot, rows, h] = attn[ROWS * n : ROWS * (n + 1)]
                    ogq[j, slot, rows, h] = gq[ROWS * n : ROWS * (n + 1)]
                for ref, value in ((odk, dkp), (odv, dvp)):
                    if t == 0:
                        ref[slot, 0:256, kv] += value
                    else:
                        ref[slot, 0:128, kv] += value[:128]
                        ref[slot, late, kv] += value[128:]

        exchange(None, lambda n, j=j: a_odd(n, j))

    def odd_partials():
        for t in range(8):
            rows = slice(ROWS * t, ROWS * (t + 1))
            opk[t % SIDE, :, t // SIDE] = (odk[:, rows] * SCALE).astype(jnp.bfloat16)
            opv[t % SIDE, :, t // SIDE] = odv[:, rows].astype(jnp.bfloat16)
        far = (x + 2) % SIDE
        for n, (op, rt, rp) in enumerate(((opk, rtk, rpk), (opv, rtv, rpv))):
            for side, step in enumerate((1, 3)):
                near_x, device = along_x(step)
                send(op.at[far, side], rt.at[side], s_rs.at[n], r_rt.at[n], device)
                send(op.at[near_x, 1 - side], rp.at[side, 1 - side], s_rs.at[n], r_rs.at[n], device)

    def even_ready():
        @pl.when(hi == 1)
        def _():
            wait(ek.at[first, :], r_fwd.at[0])
            wait(ev.at[first, :], r_fwd.at[1])

    def even_chunk(j):
        wait(eq[j], r_eq.at[j])
        wait(eg[j], r_eg.at[j])
        g = j // 2
        kv = slice(HEAD * g, HEAD * (g + 1))
        heads = [slice(0, HEAD), slice(HEAD, 2 * HEAD)]
        for b in range(4):

            @pl.when(hi == b // 2)
            def _(b=b, j=j, kv=kv, heads=heads):
                blocks = COLUMN_BLOCKS[b]
                rows = slice(BLOCK * (b % 2), BLOCK * (b % 2 + 1))
                queries = jnp.concatenate([eq[j][rows, h] for h in heads], axis=0)
                grads = jnp.concatenate([eg[j][rows, h] for h in heads], axis=0)
                keys = jnp.concatenate([ek[BLOCK * n : BLOCK * (n + 1), kv] for n in blocks], axis=0)
                values = jnp.concatenate([ev[BLOCK * n : BLOCK * (n + 1), kv] for n in blocks], axis=0)
                mask = ebias[BIAS_START[b] : BIAS_START[b] + BLOCK * len(blocks), :]
                attn, gq, dkp, dvp = attend(
                    queries, grads, keys, values, jnp.concatenate([mask] * 2, axis=1)
                )
                for n, h in enumerate(heads):
                    ea[j, rows, h] = attn[BLOCK * n : BLOCK * (n + 1)]
                    egq[j, rows, h] = gq[BLOCK * n : BLOCK * (n + 1)]
                for ref, value in ((edk, dkp), (edv, dvp)):
                    for n, cb in enumerate(blocks):
                        ref[BLOCK * cb : BLOCK * (cb + 1), kv] += value[BLOCK * n : BLOCK * (n + 1)]

        if j % 2 == 1:

            @pl.when(hi == 1)
            def _(g=g, kv=kv):
                esk[g] = (edk[0:256, kv] * SCALE).astype(jnp.bfloat16)
                esv[g] = edv[0:256, kv].astype(jnp.bfloat16)
                send(esk.at[g], erk.at[g], s_ep.at[0, g], r_ep.at[0, g], across(0))
                send(esv.at[g], erv.at[g], s_ep.at[1, g], r_ep.at[1, g], across(0))

        exchange(lambda n, j=j: a_even(n, j))

    def odd_relay():
        for n, (ref, rt, ct, rp, scale) in enumerate(
            ((odk, rtk, ctk, rpk, SCALE), (odv, rtv, ctv, rpv, 1.0))
        ):
            wait(rt, r_rt.at[n])
            for side, step in enumerate((1, 3)):
                near_x, device = along_x(step)
                for t in range(2):
                    rows = at((SIDE * t + near_x) * ROWS, ROWS)
                    ct[side, t] = (
                        ref[side, rows, :] * scale + rt[side, t].astype(jnp.float32)
                    ).astype(jnp.bfloat16)
                send(ct.at[side], rp.at[side, side], s_ct.at[n], r_rs.at[n], device)

    def odd_final():
        wait(rpk, r_rs.at[0])
        wait(rpv, r_rs.at[1])
        for t in range(2):
            rows = at((SIDE * t + x) * ROWS, ROWS)
            others = [ref[n, :, t].astype(jnp.float32) for ref in (rpk, rpv) for n in range(2)]
            ogk[:, t] = (odk[:, rows, :] * SCALE + others[0] + others[1]).astype(
                jnp.bfloat16
            )
            ogv[:, t] = (odv[:, rows, :] + others[2] + others[3]).astype(jnp.bfloat16)
        exchange(None, kv_odd_out)

    even_ready()
    even_chunk(0)
    even_chunk(1)
    odd_ready()
    odd_chunk(0)
    odd_chunk(1)
    odd_partials()
    even_chunk(2)
    odd_relay()
    even_chunk(3)
    odd_final()

    @pl.when(hi == 0)
    def _():
        for g in range(2):
            kv = slice(HEAD * g, HEAD * (g + 1))
            wait(erk.at[g], r_ep.at[0, g])
            wait(erv.at[g], r_ep.at[1, g])
            egk[:, kv] = (edk[0:256, kv] * SCALE + erk[g].astype(jnp.float32)).astype(jnp.bfloat16)
            egv[:, kv] = (edv[0:256, kv] + erv[g].astype(jnp.float32)).astype(jnp.bfloat16)

    @pl.when(hi == 1)
    def _():
        egk[...] = (edk[256:512] * SCALE).astype(jnp.bfloat16)
        egv[...] = edv[256:512].astype(jnp.bfloat16)

    exchange(kv_even_out)

    three = 3 * ROWS
    for j in range(E_CHUNKS):
        wait(eq[j].at[0:three, :], s_eq.at[j])
        wait(eg[j].at[0:three, :], s_eg.at[j])
        wait(ea.at[j, 0:three, :], s_ea.at[j])
        wait(egq.at[j, 0:three, :], s_egq.at[j])
    for j in range(O_CHUNKS):
        wait(oq[j].at[:, 0 : three // 2, :], s_oq.at[j])
        wait(og[j].at[:, 0 : three // 2, :], s_og.at[j])
        wait(oa.at[j, :, 0 : three // 2, :], s_oa.at[j])
        wait(ogq.at[j, :, 0 : three // 2, :], s_ogq.at[j])
    for n in range(4):
        wait(ek.at[0:three, :], s_kv.at[n])
        wait(ek.at[0:three, :], s_gkv.at[n])
    for n in range(2):
        wait(ok.at[:, 0 : 4 * ROWS, :], s_all.at[n])
        wait(ok.at[:, 0 : 2 * ROWS, :], s_rel.at[n])
        wait(opk.at[0:2], s_rs.at[n])
        wait(ctk, s_ct.at[n])

    @pl.when(hi == 0)
    def _():
        for n in range(2):
            wait(ek.at[first, :], s_fwd.at[n])

    @pl.when(hi == 1)
    def _():
        for n in range(2):
            for g in range(2):
                wait(esk.at[g], s_ep.at[n, g])

    for n, ref in enumerate((attn_out, gq_out, gk_out, gv_out)):
        wait(ref, r_out.at[n])


def finish_kernel(*refs):
    ins, outs, sem = refs[:4], refs[4:8], refs[8]
    for n in range(4):
        pltpu.make_async_copy(ins[n], outs[n], sem.at[n]).start()
    for n in range(4):
        pltpu.make_async_copy(ins[n], outs[n], sem.at[n]).wait()


def finish(arrays):
    anywhere = pl.BlockSpec(memory_space=pl.ANY)
    return pl.pallas_call(
        finish_kernel,
        out_shape=tuple(jax.ShapeDtypeStruct(a.shape, a.dtype) for a in arrays),
        in_specs=[anywhere] * 4,
        out_specs=(anywhere,) * 4,
        scratch_shapes=[pltpu.SemaphoreType.DMA((4,))],
    )(*[pltpu.with_memory_space_constraint(x, pltpu.VMEM) for x in arrays])


def shards(query_proj, key_proj, value_proj, grad_attn, doc_lengths, mask_tiles, pair_flags):
    bf16, f32 = jnp.bfloat16, jnp.float32
    dma, vmem = pltpu.SemaphoreType.DMA, pltpu.VMEM
    anywhere = pl.BlockSpec(memory_space=pl.ANY)
    scalars = (doc_lengths.T, jnp.transpose(mask_tiles, (1, 2, 0)), pair_flags)
    rows = SIDE * ROWS
    even_kv, odd_kv = vmem((LENGTH, PAIR), bf16), vmem((2, LENGTH, PAIR), bf16)
    even_a = vmem((E_CHUNKS, rows, E_WIDTH), bf16)
    odd_a = vmem((O_CHUNKS, 2, 2 * ROWS, O_WIDTH), bf16)
    even_d, odd_d = vmem((LENGTH, PAIR), f32), vmem((2, LENGTH, PAIR), f32)
    even_part, even_g = vmem((2, rows, HEAD), bf16), vmem((rows, PAIR), bf16)
    odd_part, odd_recv = vmem((4, 2, 2, ROWS, PAIR), bf16), vmem((2, 2, 2, ROWS, PAIR), bf16)
    odd_g = vmem((2, 2, ROWS, PAIR), bf16)
    return finish(pl.pallas_call(
        kernel,
        out_shape=tuple(
            jax.ShapeDtypeStruct(a.shape, bf16)
            for a in (query_proj, query_proj, key_proj, value_proj)
        ),
        in_specs=[anywhere] * 7,
        out_specs=(anywhere,) * 4,
        scratch_shapes=[
            even_kv, even_kv, odd_kv, odd_kv, even_a, even_a, odd_a, odd_a,
            even_d, even_d, odd_d, odd_d,
            vmem((6 * BLOCK, BLOCK), f32), vmem((2, 576, BLOCK), f32),
            even_part, even_part, even_part, even_part, even_g, even_g,
            odd_part, odd_part, odd_recv, odd_recv, odd_g, odd_g,
            odd_g, odd_g, odd_g, odd_g, dma((2,)), dma((2,)),
            *[pltpu.SMEM(a.shape, a.dtype) for a in scalars], dma((3,)),
            dma((E_CHUNKS,)), dma((E_CHUNKS,)), dma((O_CHUNKS,)), dma((O_CHUNKS,)),
            dma((4,)), dma((4,)), dma((2,)), dma((2, 2)), dma((2,)), dma((4,)), dma((4,)), dma((2,)),
            dma((E_CHUNKS,)), dma((E_CHUNKS,)), dma((O_CHUNKS,)), dma((O_CHUNKS,)),
            dma((4,)), dma((2,)), dma((2,)), dma((2, 2)), dma((2,)),
            dma((E_CHUNKS,)), dma((E_CHUNKS,)), dma((O_CHUNKS,)), dma((O_CHUNKS,)), dma((4,)),
            *[vmem((rows, E_WIDTH), bf16)] * (2 * E_CHUNKS),
            *[vmem((2, 2 * ROWS, O_WIDTH), bf16)] * (2 * O_CHUNKS),
        ],
        compiler_params=pltpu.CompilerParams(
            collective_id=0, has_side_effects=True, vmem_limit_bytes=48 * 2**20
        ),
    )(*[
        pltpu.with_memory_space_constraint(x, pltpu.HBM)
        for x in (query_proj, key_proj, value_proj, grad_attn, *scalars)
    ]))


def solution(mesh):
    split = P("dp", "ctx", None)
    return jax.shard_map(
        shards,
        mesh=mesh,
        in_specs=(split,) * 4 + (P(),) * 3,
        out_specs=(split,) * 4,
        check_vma=False,
    )
```

```python
import functools
import math

import jax
import jax.numpy as jnp
from jax import lax
from jax.experimental import pallas as pl
from jax.experimental.pallas import tpu as pltpu
from jax.sharding import PartitionSpec as P

MESH = pl.DeviceIdType.MESH
HEAD = 128
RATIO = 4
ROWS = 64
LENGTH = 512
BLOCK = 128
SIDE = 4
PAIR = 2 * HEAD
QPAIR = RATIO * PAIR
E_CHUNKS = 4
E_WIDTH = QPAIR // E_CHUNKS
O_CHUNKS = 2
O_WIDTH = QPAIR // O_CHUNKS
SCALE = HEAD ** (-0.5)
EXP2_SCALE = SCALE / math.log(2.0)
COLUMN_BLOCKS = ((0,), (0, 1), (0, 1, 2), (0, 2, 3))
BIAS_START = (0, 128, 0, 384)
NT_DIMS = (((1,), (1,)), ((), ()))
TN_DIMS = (((0,), (0,)), ((), ()))
NN_DIMS = (((1,), (0,)), ((), ()))
STEPS = (1, 3, 2)


def mm(a, b, dims):
    return lax.dot_general(a, b, dims, preferred_element_type=jnp.float32)


def attend(queries, grads, keys, values, mask):
    scores = mm(keys, queries, NT_DIMS) + mask
    peak = jnp.max(scores, axis=0, keepdims=True)
    expd = jnp.exp2((scores - peak) * EXP2_SCALE)
    probs = expd * (1.0 / jnp.sum(expd, axis=0, keepdims=True))
    probs_b = probs.astype(jnp.bfloat16)
    dprobs = mm(values, grads, NT_DIMS)
    delta = jnp.sum(probs * dprobs, axis=0, keepdims=True)
    dscores = (probs * (dprobs - delta)).astype(jnp.bfloat16)
    attn = mm(probs_b, values, TN_DIMS).astype(jnp.bfloat16)
    gq = (mm(dscores, keys, TN_DIMS) * SCALE).astype(jnp.bfloat16)
    return attn, gq, mm(dscores, queries, NN_DIMS), mm(probs_b, grads, NN_DIMS)


def kernel(
    q_in, k_in, v_in, g_in, lengths_in, tiles_in, flags_in,
    attn_out, gq_out, gk_out, gv_out,
    ek, ev, ok, ov, ea, egq, oa, ogq, edk, edv, odk, odv, ebias, obias,
    esk, esv, erk, erv, egk, egv, opk, opv, rpk, rpv, ogk, ogv, rtk, rtv, ctk, ctv, r_rt, s_ct,
    lengths, tiles, flags, scalar_sem,
    r_eq, r_eg, r_oq, r_og, r_kv, r_all, r_fwd, r_ep, r_rs, r_out, r_rel, s_rel,
    s_eq, s_eg, s_oq, s_og, s_kv, s_all, s_fwd, s_ep, s_rs,
    s_ea, s_egq, s_oa, s_ogq, s_gkv,
    *bufs,
):
    eq, eg = bufs[0:E_CHUNKS], bufs[E_CHUNKS : 2 * E_CHUNKS]
    oq, og = bufs[2 * E_CHUNKS : 2 * E_CHUNKS + O_CHUNKS], bufs[2 * E_CHUNKS + O_CHUNKS :]
    dp = lax.axis_index("dp")
    c = lax.axis_index("ctx")
    half = lax.axis_size("dp") // 2
    low = dp // half
    zc = dp % half
    hi = c // SIDE
    x = c % SIDE
    y = 2 * hi + low

    def along_x(step):
        xn = (x + step) % SIDE
        return xn, {"dp": dp, "ctx": hi * SIDE + xn}

    def along_y(step):
        yn = (y + step) % SIDE
        return yn, {"dp": (yn % 2) * half + zc, "ctx": (yn // 2) * SIDE + x}

    def across(device_hi):
        return {"dp": dp, "ctx": device_hi * SIDE + x}

    scalar_copies = [
        pltpu.make_async_copy(src, dst, scalar_sem.at[n])
        for n, (src, dst) in enumerate(((lengths_in, lengths), (tiles_in, tiles), (flags_in, flags)))
    ]
    for copy in scalar_copies:
        copy.start()

    barrier = pltpu.get_barrier_semaphore()
    for step in STEPS:
        for along in (along_x, along_y):
            pl.semaphore_signal(barrier, inc=1, device_id=along(step)[1], device_id_type=MESH)
    pl.semaphore_wait(barrier, 6)

    def send(src, dst, send_sem, recv_sem, device):
        pltpu.make_async_remote_copy(
            src_ref=src, dst_ref=dst, send_sem=send_sem, recv_sem=recv_sem,
            device_id=device, device_id_type=MESH,
        ).start()

    def keep(src, dst, _, recv_sem):
        pltpu.make_async_copy(src, dst, recv_sem).start()

    def wait(ref, sem):
        pltpu.make_async_copy(ref, ref, sem).wait()

    def at(start, size):
        return pl.ds(pl.multiple_of(start, size), size)

    rows_c = at(c * ROWS, ROWS)
    rows_x = at(x * ROWS, ROWS)
    rows_hi = at(hi * ROWS, ROWS)

    def kv_even(n):
        cols = at(n * PAIR, PAIR)
        return [
            (k_in.at[0, :, cols], ek.at[rows_c, :], s_kv.at[0], r_kv.at[0]),
            (v_in.at[0, :, cols], ev.at[rows_c, :], s_kv.at[1], r_kv.at[1]),
        ]

    def kv_odd(n):
        cols = at(n * PAIR, PAIR)
        return [
            (k_in.at[1, :, cols], ok.at[low, rows_c, :], s_kv.at[2], r_kv.at[2]),
            (v_in.at[1, :, cols], ov.at[low, rows_c, :], s_kv.at[3], r_kv.at[3]),
        ]

    def q_even(n, j):
        cols = at(n * QPAIR + j * E_WIDTH, E_WIDTH)
        return [
            (q_in.at[0, :, cols], eq[j].at[rows_x, :], s_eq.at[j], r_eq.at[j]),
            (g_in.at[0, :, cols], eg[j].at[rows_x, :], s_eg.at[j], r_eg.at[j]),
        ]

    def q_odd(n, j):
        cols = at(n * QPAIR + j * O_WIDTH, O_WIDTH)
        return [
            (q_in.at[1, :, cols], oq[j].at[low, rows_hi, :], s_oq.at[j], r_oq.at[j]),
            (g_in.at[1, :, cols], og[j].at[low, rows_hi, :], s_og.at[j], r_og.at[j]),
        ]

    def exchange(even=None, odd=None):
        for step in STEPS:
            if odd is not None:
                n, device = along_y(step)
                for item in odd(n):
                    send(*item, device)
            if even is not None:
                n, device = along_x(step)
                for item in even(n):
                    send(*item, device)
        for item in (odd(y) if odd is not None else []) + (even(x) if even is not None else []):
            keep(*item)

    exchange(kv_even, kv_odd)
    exchange(lambda n: q_even(n, 0))

    for copy in scalar_copies:
        copy.wait()
    flag = jnp.where(flags[dp] == 1, 1, 0)
    lane = lax.broadcasted_iota(jnp.int32, (BLOCK, BLOCK), 1)
    sub = lax.broadcasted_iota(jnp.int32, (BLOCK, BLOCK), 0)

    def segment_ends(seq):
        ends = []
        total = lengths[0, seq]
        for d in range(1, 8):
            ends.append(total)
            total = total + lengths[d, seq]
        return ends

    def addend(ends, row, col, tile):
        row_doc = sum((row >= e).astype(jnp.int32) for e in ends)
        col_doc = sum((col >= e).astype(jnp.int32) for e in ends)
        allowed = (col <= row) & ((col_doc == row_doc) | (col_doc == 0)) & (tile == 1)
        return jnp.where(allowed, 0.0, -1e30)

    wait(ok.at[:, 0 : 2 * ROWS, :], r_kv.at[2])
    wait(ov.at[:, 0 : 2 * ROWS, :], r_kv.at[3])
    for side, step in enumerate((1, 3)):
        _, device = along_x(step)
        for t in range(2):
            part = at((SIDE * t + x) * ROWS, ROWS)
            for n, ref in enumerate((ok, ov)):
                here = ref.at[:, part, :]
                send(here, here, s_all.at[n], r_all.at[2 * side + n], device)
    wait(ek.at[0 : SIDE * ROWS, :], r_kv.at[0])
    wait(ev.at[0 : SIDE * ROWS, :], r_kv.at[1])

    first = pl.ds(0, SIDE * ROWS)

    @pl.when(hi == 0)
    def _():
        for n, ref in enumerate((ek, ev)):
            send(ref.at[first, :], ref.at[first, :], s_fwd.at[n], r_fwd.at[n], across(1))

    exchange(lambda n: q_even(n, 1), lambda n: q_odd(n, 0))

    for b in range(4):

        @pl.when(hi == b // 2)
        def _(b=b):
            seq = 2 * dp
            ends = segment_ends(seq)
            row = lane + BLOCK * b
            for n, cb in enumerate(COLUMN_BLOCKS[b]):
                top, bottom = (
                    jnp.where(
                        lane < 64,
                        tiles[2 * b, 2 * cb + m, seq],
                        tiles[2 * b + 1, 2 * cb + m, seq],
                    )
                    for m in range(2)
                )
                start = BIAS_START[b] + BLOCK * n
                ebias[start : start + BLOCK, :] = addend(
                    ends, row, sub + BLOCK * cb, jnp.where(sub < 64, top, bottom)
                )

    for side, step in enumerate((1, 3)):
        _, device = along_x(step)
        for n, ref in enumerate((ok, ov)):
            wait(ref.at[:, 0 : 2 * ROWS, :], r_all.at[2 * side + n])
            for t in range(2):
                part = at((SIDE * t + (x + 4 - step) % SIDE) * ROWS, ROWS)
                here = ref.at[side, part, :]
                send(here, here, s_rel.at[n], r_rel.at[2 * side + n], device)

    exchange(lambda n: q_even(n, 2), lambda n: q_odd(n, 1))
    exchange(lambda n: q_even(n, 3))

    def source(slot):
        return slot + flag - 2 * slot * flag

    near = x + 2

    @pl.loop(0, 2)
    def _(slot):
        seq = 2 * (source(slot) * half + zc) + 1
        ends = segment_ends(seq)
        inner = lane % ROWS
        for t, start in ((0, 0), (0, BLOCK), (1, 2 * BLOCK)):
            row_tile = SIDE * t + x
            cb = start // BLOCK % 2
            tile = jnp.where(sub < 64, tiles[row_tile, 2 * cb, seq], tiles[row_tile, 2 * cb + 1, seq])
            obias[slot, start : start + BLOCK, :] = addend(
                ends, inner + row_tile * ROWS, sub + BLOCK * cb, tile
            )
        for m in range(3):
            start = 3 * BLOCK + ROWS * m
            tile = jnp.zeros_like(sub[:ROWS]) + tiles[SIDE + x, near + m, seq]
            obias[slot, start : start + ROWS, :] = addend(
                ends, inner[:ROWS] + (SIDE + x) * ROWS, sub[:ROWS] + (near + m) * ROWS, tile
            )

    for ref in (edk, edv, odk, odv):
        ref[...] = jnp.zeros_like(ref)

    def a_even(n, j):
        rows, cols = at(n * ROWS, ROWS), at(x * QPAIR + j * E_WIDTH, E_WIDTH)
        return [
            (ea.at[j, rows, :], attn_out.at[0, :, cols], s_ea.at[j], r_out.at[0]),
            (egq.at[j, rows, :], gq_out.at[0, :, cols], s_egq.at[j], r_out.at[1]),
        ]

    def a_odd(n, j):
        rows, cols = at((n // 2) * ROWS, ROWS), at(y * QPAIR + j * O_WIDTH, O_WIDTH)
        return [
            (oa.at[j, n % 2, rows, :], attn_out.at[1, :, cols], s_oa.at[j], r_out.at[0]),
            (ogq.at[j, n % 2, rows, :], gq_out.at[1, :, cols], s_ogq.at[j], r_out.at[1]),
        ]

    def kv_even_out(n):
        rows, cols = at(n * ROWS, ROWS), at(x * PAIR, PAIR)
        return [
            (egk.at[rows, :], gk_out.at[0, :, cols], s_gkv.at[0], r_out.at[2]),
            (egv.at[rows, :], gv_out.at[0, :, cols], s_gkv.at[1], r_out.at[3]),
        ]

    def kv_odd_out(n):
        cols = at(y * PAIR, PAIR)
        return [
            (ogk.at[n % 2, n // 2], gk_out.at[1, :, cols], s_gkv.at[2], r_out.at[2]),
            (ogv.at[n % 2, n // 2], gv_out.at[1, :, cols], s_gkv.at[3], r_out.at[3]),
        ]

    late = pl.ds(pl.multiple_of(near * ROWS, ROWS), 3 * ROWS)
    def odd_ready():
        for side in range(2):
            for n, ref in enumerate((ok, ov)):
                wait(ref.at[side, 0 : 2 * ROWS, :], r_rel.at[2 * side + n])

    def odd_chunk(j):
        wait(oq[j], r_oq.at[j])
        wait(og[j], r_og.at[j])
        kv = slice(HEAD * j, HEAD * (j + 1))
        heads = [slice(HEAD * h, HEAD * (h + 1)) for h in range(RATIO)]

        @pl.loop(0, 2)
        def _(slot, j=j, kv=kv, heads=heads):
            u = source(slot)
            for t in range(2):
                rows = slice(ROWS * t, ROWS * (t + 1))
                queries = jnp.concatenate([oq[j][u, rows, h] for h in heads], axis=0)
                grads = jnp.concatenate([og[j][u, rows, h] for h in heads], axis=0)
                if t == 0:
                    keys, values = ok[u, 0:256, kv], ov[u, 0:256, kv]
                    mask = obias[slot, 0:256, :]
                else:
                    keys = jnp.concatenate([ok[u, 0:128, kv], ok[u, late, kv]], axis=0)
                    values = jnp.concatenate([ov[u, 0:128, kv], ov[u, late, kv]], axis=0)
                    mask = obias[slot, 256:576, :]
                attn, gq, dkp, dvp = attend(
                    queries, grads, keys, values, jnp.concatenate([mask] * 2, axis=1)
                )
                for n, h in enumerate(heads):
                    oa[j, slot, rows, h] = attn[ROWS * n : ROWS * (n + 1)]
                    ogq[j, slot, rows, h] = gq[ROWS * n : ROWS * (n + 1)]
                for ref, value in ((odk, dkp), (odv, dvp)):
                    if t == 0:
                        ref[slot, 0:256, kv] += value
                    else:
                        ref[slot, 0:128, kv] += value[:128]
                        ref[slot, late, kv] += value[128:]

        exchange(None, lambda n, j=j: a_odd(n, j))

    def odd_partials():
        for t in range(8):
            rows = slice(ROWS * t, ROWS * (t + 1))
            opk[t % SIDE, :, t // SIDE] = (odk[:, rows] * SCALE).astype(jnp.bfloat16)
            opv[t % SIDE, :, t // SIDE] = odv[:, rows].astype(jnp.bfloat16)
        far = (x + 2) % SIDE
        for n, (op, rt, rp) in enumerate(((opk, rtk, rpk), (opv, rtv, rpv))):
            for side, step in enumerate((1, 3)):
                near_x, device = along_x(step)
                send(op.at[far, side], rt.at[side], s_rs.at[n], r_rt.at[n], device)
                send(op.at[near_x, 1 - side], rp.at[side, 1 - side], s_rs.at[n], r_rs.at[n], device)

    def even_ready():
        @pl.when(hi == 1)
        def _():
            wait(ek.at[first, :], r_fwd.at[0])
            wait(ev.at[first, :], r_fwd.at[1])

    def even_chunk(j):
        wait(eq[j], r_eq.at[j])
        wait(eg[j], r_eg.at[j])
        g = j // 2
        kv = slice(HEAD * g, HEAD * (g + 1))
        heads = [slice(0, HEAD), slice(HEAD, 2 * HEAD)]
        for b in range(4):

            @pl.when(hi == b // 2)
            def _(b=b, j=j, kv=kv, heads=heads):
                blocks = COLUMN_BLOCKS[b]
                rows = slice(BLOCK * (b % 2), BLOCK * (b % 2 + 1))
                queries = jnp.concatenate([eq[j][rows, h] for h in heads], axis=0)
                grads = jnp.concatenate([eg[j][rows, h] for h in heads], axis=0)
                keys = jnp.concatenate([ek[BLOCK * n : BLOCK * (n + 1), kv] for n in blocks], axis=0)
                values = jnp.concatenate([ev[BLOCK * n : BLOCK * (n + 1), kv] for n in blocks], axis=0)
                mask = ebias[BIAS_START[b] : BIAS_START[b] + BLOCK * len(blocks), :]
                attn, gq, dkp, dvp = attend(
                    queries, grads, keys, values, jnp.concatenate([mask] * 2, axis=1)
                )
                for n, h in enumerate(heads):
                    ea[j, rows, h] = attn[BLOCK * n : BLOCK * (n + 1)]
                    egq[j, rows, h] = gq[BLOCK * n : BLOCK * (n + 1)]
                for ref, value in ((edk, dkp), (edv, dvp)):
                    for n, cb in enumerate(blocks):
                        ref[BLOCK * cb : BLOCK * (cb + 1), kv] += value[BLOCK * n : BLOCK * (n + 1)]

        if j % 2 == 1:

            @pl.when(hi == 1)
            def _(g=g, kv=kv):
                esk[g] = (edk[0:256, kv] * SCALE).astype(jnp.bfloat16)
                esv[g] = edv[0:256, kv].astype(jnp.bfloat16)
                send(esk.at[g], erk.at[g], s_ep.at[0, g], r_ep.at[0, g], across(0))
                send(esv.at[g], erv.at[g], s_ep.at[1, g], r_ep.at[1, g], across(0))

        exchange(lambda n, j=j: a_even(n, j))

    def odd_relay():
        for n, (ref, rt, ct, rp, scale) in enumerate(
            ((odk, rtk, ctk, rpk, SCALE), (odv, rtv, ctv, rpv, 1.0))
        ):
            wait(rt, r_rt.at[n])
            for side, step in enumerate((1, 3)):
                near_x, device = along_x(step)
                for t in range(2):
                    rows = at((SIDE * t + near_x) * ROWS, ROWS)
                    ct[side, t] = (
                        ref[side, rows, :] * scale + rt[side, t].astype(jnp.float32)
                    ).astype(jnp.bfloat16)
                send(ct.at[side], rp.at[side, side], s_ct.at[n], r_rs.at[n], device)

    def odd_final():
        wait(rpk, r_rs.at[0])
        wait(rpv, r_rs.at[1])
        for t in range(2):
            rows = at((SIDE * t + x) * ROWS, ROWS)
            others = [ref[n, :, t].astype(jnp.float32) for ref in (rpk, rpv) for n in range(2)]
            ogk[:, t] = (odk[:, rows, :] * SCALE + others[0] + others[1]).astype(
                jnp.bfloat16
            )
            ogv[:, t] = (odv[:, rows, :] + others[2] + others[3]).astype(jnp.bfloat16)
        exchange(None, kv_odd_out)

    even_ready()
    even_chunk(0)
    even_chunk(1)
    odd_ready()
    odd_chunk(0)
    odd_chunk(1)
    odd_partials()
    even_chunk(2)
    odd_relay()
    even_chunk(3)
    odd_final()

    @pl.when(hi == 0)
    def _():
        for g in range(2):
            kv = slice(HEAD * g, HEAD * (g + 1))
            wait(erk.at[g], r_ep.at[0, g])
            wait(erv.at[g], r_ep.at[1, g])
            egk[:, kv] = (edk[0:256, kv] * SCALE + erk[g].astype(jnp.float32)).astype(jnp.bfloat16)
            egv[:, kv] = (edv[0:256, kv] + erv[g].astype(jnp.float32)).astype(jnp.bfloat16)

    @pl.when(hi == 1)
    def _():
        egk[...] = (edk[256:512] * SCALE).astype(jnp.bfloat16)
        egv[...] = edv[256:512].astype(jnp.bfloat16)

    exchange(kv_even_out)

    three = 3 * ROWS
    for j in range(E_CHUNKS):
        wait(eq[j].at[0:three, :], s_eq.at[j])
        wait(eg[j].at[0:three, :], s_eg.at[j])
        wait(ea.at[j, 0:three, :], s_ea.at[j])
        wait(egq.at[j, 0:three, :], s_egq.at[j])
    for j in range(O_CHUNKS):
        wait(oq[j].at[:, 0 : three // 2, :], s_oq.at[j])
        wait(og[j].at[:, 0 : three // 2, :], s_og.at[j])
        wait(oa.at[j, :, 0 : three // 2, :], s_oa.at[j])
        wait(ogq.at[j, :, 0 : three // 2, :], s_ogq.at[j])
    for n in range(4):
        wait(ek.at[0:three, :], s_kv.at[n])
        wait(ek.at[0:three, :], s_gkv.at[n])
    for n in range(2):
        wait(ok.at[:, 0 : 4 * ROWS, :], s_all.at[n])
        wait(ok.at[:, 0 : 2 * ROWS, :], s_rel.at[n])
        wait(opk.at[0:2], s_rs.at[n])
        wait(ctk, s_ct.at[n])

    @pl.when(hi == 0)
    def _():
        for n in range(2):
            wait(ek.at[first, :], s_fwd.at[n])

    @pl.when(hi == 1)
    def _():
        for n in range(2):
            for g in range(2):
                wait(esk.at[g], s_ep.at[n, g])

    for n, ref in enumerate((attn_out, gq_out, gk_out, gv_out)):
        wait(ref, r_out.at[n])


def finish_kernel(*refs):
    ins, outs, sem = refs[:4], refs[4:8], refs[8]
    for n in range(4):
        pltpu.make_async_copy(ins[n], outs[n], sem.at[n]).start()
    for n in range(4):
        pltpu.make_async_copy(ins[n], outs[n], sem.at[n]).wait()


def finish(arrays):
    anywhere = pl.BlockSpec(memory_space=pl.ANY)
    return pl.pallas_call(
        finish_kernel,
        out_shape=tuple(jax.ShapeDtypeStruct(a.shape, a.dtype) for a in arrays),
        in_specs=[anywhere] * 4,
        out_specs=(anywhere,) * 4,
        scratch_shapes=[pltpu.SemaphoreType.DMA((4,))],
    )(*[pltpu.with_memory_space_constraint(x, pltpu.VMEM) for x in arrays])


def shards(query_proj, key_proj, value_proj, grad_attn, doc_lengths, mask_tiles, pair_flags):
    bf16, f32 = jnp.bfloat16, jnp.float32
    dma, vmem = pltpu.SemaphoreType.DMA, pltpu.VMEM
    anywhere = pl.BlockSpec(memory_space=pl.ANY)
    scalars = (doc_lengths.T, jnp.transpose(mask_tiles, (1, 2, 0)), pair_flags)
    rows = SIDE * ROWS
    even_kv, odd_kv = vmem((LENGTH, PAIR), bf16), vmem((2, LENGTH, PAIR), bf16)
    even_a = vmem((E_CHUNKS, rows, E_WIDTH), bf16)
    odd_a = vmem((O_CHUNKS, 2, 2 * ROWS, O_WIDTH), bf16)
    even_d, odd_d = vmem((LENGTH, PAIR), f32), vmem((2, LENGTH, PAIR), f32)
    even_part, even_g = vmem((2, rows, HEAD), bf16), vmem((rows, PAIR), bf16)
    odd_part, odd_recv = vmem((4, 2, 2, ROWS, PAIR), bf16), vmem((2, 2, 2, ROWS, PAIR), bf16)
    odd_g = vmem((2, 2, ROWS, PAIR), bf16)
    return finish(pl.pallas_call(
        kernel,
        out_shape=tuple(
            jax.ShapeDtypeStruct(a.shape, bf16)
            for a in (query_proj, query_proj, key_proj, value_proj)
        ),
        in_specs=[anywhere] * 7,
        out_specs=(anywhere,) * 4,
        scratch_shapes=[
            even_kv, even_kv, odd_kv, odd_kv, even_a, even_a, odd_a, odd_a,
            even_d, even_d, odd_d, odd_d,
            vmem((6 * BLOCK, BLOCK), f32), vmem((2, 576, BLOCK), f32),
            even_part, even_part, even_part, even_part, even_g, even_g,
            odd_part, odd_part, odd_recv, odd_recv, odd_g, odd_g,
            odd_g, odd_g, odd_g, odd_g, dma((2,)), dma((2,)),
            *[pltpu.SMEM(a.shape, a.dtype) for a in scalars], dma((3,)),
            dma((E_CHUNKS,)), dma((E_CHUNKS,)), dma((O_CHUNKS,)), dma((O_CHUNKS,)),
            dma((4,)), dma((4,)), dma((2,)), dma((2, 2)), dma((2,)), dma((4,)), dma((4,)), dma((2,)),
            dma((E_CHUNKS,)), dma((E_CHUNKS,)), dma((O_CHUNKS,)), dma((O_CHUNKS,)),
            dma((4,)), dma((2,)), dma((2,)), dma((2, 2)), dma((2,)),
            dma((E_CHUNKS,)), dma((E_CHUNKS,)), dma((O_CHUNKS,)), dma((O_CHUNKS,)), dma((4,)),
            *[vmem((rows, E_WIDTH), bf16)] * (2 * E_CHUNKS),
            *[vmem((2, 2 * ROWS, O_WIDTH), bf16)] * (2 * O_CHUNKS),
        ],
        compiler_params=pltpu.CompilerParams(
            collective_id=0, has_side_effects=True, vmem_limit_bytes=48 * 2**20
        ),
    )(*[
        pltpu.with_memory_space_constraint(x, pltpu.HBM)
        for x in (query_proj, key_proj, value_proj, grad_attn, *scalars)
    ]))


def solution(mesh):
    split = P("dp", "ctx", None)
    return jax.shard_map(
        shards,
        mesh=mesh,
        in_specs=(split,) * 4 + (P(),) * 3,
        out_specs=(split,) * 4,
        check_vma=False,
    )
```
